32 devices in a mesh: cfg: 2 (over y), tm: 4 (over z), space: 2 (over x), spin: 2 (over core).
Axes of the slice: x: 2, y: 2, z: 4, core: 2. Of those that a mesh axis runs over, the one named last changes fastest.
Arguments:
- eigenvectors: bfloat16 [8, 2, 3, 16, 2, 2, 128], P(('cfg', 'tm'), None, None, 'space'), parts along dimension 0, may hold values from -6 to 6
- gauge_links: bfloat16 [8, 3, 2, 3, 3, 16, 4], P(('cfg', 'tm'), None, None, None, None, 'space'), parts along dimension 0, may hold values from -2.4375 to 2.4375
- perambulators: bfloat16 [8, 512, 1024], P(('cfg', 'tm'), ('space', 'spin')), parts along dimension 0, may hold values from -0.1875 to 0.1875
- source_times: int32 [16], replicated, may hold values from 0 to 3
- insert_offsets: int32 [4], replicated, may hold values from 0 to 2
- derivative_dirs: int32 [3], replicated, may hold values from 0 to 2, each once
Outputs:
- elementals: float32 [8, 128, 3, 2, 128], P(('cfg', 'tm'), 'space', None, None, 'spin'), parts along dimension 0
- chain_products: bfloat16 [8, 512, 1024], P(('cfg', 'tm'), ('space', 'spin')), parts along dimension 0
- correlator: float32 [32, 2], P('cfg'), parts along dimension 0
The draws below stay inside these ranges and needn't reach their ends.
There are 2 independent parts, one for each index of `cfg`. The reference program is written for one: setup_inputs(seed, part) draws one part's arguments, and reference() takes and returns one part's arrays. A program takes and returns all parts, laid end to end along the dimension named above; an argument that names none is the same for every part. Nothing has to cross between parts.
Inputs may be any that keep to these rules, and one draw needn't show every extreme that they name: `derivative_dirs`: each of 0, 1, 2 appears once.
All inputs are finite; a program needn't handle non-finite values.
Results may differ from the reference program's by a relative error of at most 0.012.
Values may be sent and summed in bfloat16 or wider, within the bound.
A program may use at most 64 MiB of HBM per device.

```python
import math
import jax
import jax.numpy as jnp
import numpy as np
from jax import lax

MODES = 128
ORDER = 512
SIDE = 2
DEPTH = 16
TIMES = 4
SOURCES = 16
INSERTS = 4


def plant(values, key, low, largest):
    extent = values.shape
    index_at = [jax.random.randint(jax.random.fold_in(key, axis), (), 0, extent[axis]) for axis in range(len(extent))]
    values = values.at[tuple(index_at)].set(low)
    longest = extent.index(max(extent))
    index_at[longest] = (index_at[longest] + 1) % extent[longest]
    return values.at[tuple(index_at)].set(largest)


def level_of(key, dims, pieces, smallest, top_value):
    factor_of = 1.0
    for axis_at, blocks in pieces:
        heights = jax.random.uniform(jax.random.fold_in(jax.random.fold_in(key, 6), axis_at), (blocks,), jnp.float32, smallest / len(pieces), top_value / len(pieces))
        factor_of = factor_of * jnp.repeat(jnp.exp(heights), dims[axis_at] // blocks).reshape((-1,) + (1,) * (len(dims) - 1 - axis_at))
    return factor_of


def bell_draw(own_key, extent, deviation, limit, shards=(), kind=jnp.bfloat16):
    gain = level_of(own_key, extent, shards, -0.22, 0.18) if shards else 1.0
    entries = jax.random.normal(own_key, extent, jnp.float32) * deviation * gain
    return jnp.minimum(jnp.maximum(entries, -limit), limit).astype(kind)


def setup_inputs(seed: int = 0, part: int = 0) -> dict:
    keys = jax.random.split(jax.random.key(seed), 7)
    part_keys = jax.random.split(jax.random.fold_in(keys[6], part), 7)
    eigenvectors = bell_draw(part_keys[0], (TIMES, 2, 3, DEPTH, SIDE, SIDE, MODES), 1.0, 6.0, ((0, 4), (3, 2)))
    gauge_links = bell_draw(part_keys[1], (TIMES, 3, 2, 3, 3, DEPTH, SIDE * SIDE), 0.408, 2.4375, ((0, 4), (5, 2)))
    perambulators = bell_draw(part_keys[2], (TIMES, ORDER, 2 * ORDER), (2 * ORDER) ** -0.5, 0.1875, ((0, 4), (1, 4)))
    source_times = plant(jax.random.randint(keys[3], (SOURCES,), 0, TIMES), jax.random.fold_in(keys[3], 1), 0, TIMES - 1).astype(jnp.int32)
    insert_offsets = plant(jax.random.randint(keys[4], (INSERTS,), 0, 3), jax.random.fold_in(keys[4], 1), 0, 2).astype(jnp.int32)
    derivative_dirs = jax.random.permutation(keys[5], 3).astype(jnp.int32)
    return dict(eigenvectors=eigenvectors, gauge_links=gauge_links, perambulators=perambulators, source_times=source_times, insert_offsets=insert_offsets, derivative_dirs=derivative_dirs)


def gamma_tables():
    sigma_real = np.zeros((3, 2, 2), np.float32)
    sigma_imag = np.zeros((3, 2, 2), np.float32)
    sigma_real[0] = [[0.0, 1.0], [1.0, 0.0]]
    sigma_imag[1] = [[0.0, -1.0], [1.0, 0.0]]
    sigma_real[2] = [[1.0, 0.0], [0.0, -1.0]]
    gamma_real = np.zeros((3, 4, 4), np.float32)
    gamma_imag = np.zeros((3, 4, 4), np.float32)
    gamma_real[:, 0:2, 2:4] = sigma_imag
    gamma_imag[:, 0:2, 2:4] = -sigma_real
    gamma_real[:, 2:4, 0:2] = -sigma_imag
    gamma_imag[:, 2:4, 0:2] = sigma_real
    return (gamma_real, gamma_imag)

def color_product(matrix, vectors):
    return lax.optimization_barrier(jnp.sum(matrix[:, :, :, :, :, None] * vectors[None], axis=1))

def times_links(link_field, vectors):
    real_part = color_product(link_field[0], vectors[0]) - color_product(link_field[1], vectors[1])
    imag_part = color_product(link_field[0], vectors[1]) + color_product(link_field[1], vectors[0])
    return jnp.stack([real_part, imag_part])

def times_adjoint(link_field, vectors):
    swapped = jnp.swapaxes(link_field, 1, 2)
    real_part = color_product(swapped[0], vectors[0]) + color_product(swapped[1], vectors[1])
    imag_part = color_product(swapped[0], vectors[1]) - color_product(swapped[1], vectors[0])
    return jnp.stack([real_part, imag_part])

def block_matrix(real_part, imag_part):
    upper_half = jnp.concatenate([real_part, imag_part], axis=1)
    lower_half = jnp.concatenate([-imag_part, real_part], axis=1)
    return jnp.concatenate([upper_half, lower_half], axis=0)

def row_block(matrix_rows):
    matrix_order = matrix_rows.shape[1] // 2
    return block_matrix(matrix_rows[:, :matrix_order], matrix_rows[:, matrix_order:])

def operator_matrix(elementals_wide, derivative_dirs):
    gamma_real, gamma_imag = gamma_tables()
    select = (derivative_dirs[:, None] == jnp.arange(3, dtype=jnp.int32)[None, :]).astype(jnp.float32)
    mixed_real = jnp.einsum('km,kpq->mpq', select, jnp.asarray(gamma_real), precision=lax.Precision.HIGHEST)
    mixed_imag = jnp.einsum('km,kpq->mpq', select, jnp.asarray(gamma_imag), precision=lax.Precision.HIGHEST)
    elem_real = elementals_wide[:, :, 0, :]
    elem_imag = elementals_wide[:, :, 1, :]
    pattern = 'mpq,amb->paqb'
    real_part = jnp.einsum(pattern, mixed_real, elem_real, precision=lax.Precision.HIGHEST) - jnp.einsum(pattern, mixed_imag, elem_imag, precision=lax.Precision.HIGHEST)
    imag_part = jnp.einsum(pattern, mixed_real, elem_imag, precision=lax.Precision.HIGHEST) + jnp.einsum(pattern, mixed_imag, elem_real, precision=lax.Precision.HIGHEST)
    matrix_order = 4 * elementals_wide.shape[0]
    real_part = real_part.reshape((matrix_order, matrix_order)).astype(jnp.bfloat16)
    imag_part = imag_part.reshape((matrix_order, matrix_order)).astype(jnp.bfloat16)
    return block_matrix(real_part, imag_part)

def trace_pair(product):
    matrix_order = product.shape[1] // 2
    return jnp.stack([jnp.trace(product[:, :matrix_order]), jnp.trace(product[:, matrix_order:])])

def correlate(traces, source_times, insert_offsets):
    slot_count = traces.shape[0]
    counts = lax.optimization_barrier(jnp.sum((insert_offsets[:, None] == jnp.arange(3, dtype=jnp.int32)[None, :]).astype(jnp.float32), axis=0))
    weighted = lax.optimization_barrier(jnp.sum(traces * counts[None, :, None], axis=1))
    picker = (source_times[:, None] == jnp.arange(slot_count, dtype=jnp.int32)[None, :]).astype(jnp.float32)
    return jnp.dot(picker, weighted, precision=lax.Precision.HIGHEST)

def slice_elementals(vectors, link_block, norm_scale):
    depth_cells, side_cells = (vectors.shape[2], vectors.shape[3])
    mode_count = vectors.shape[5]
    vectors_wide = vectors.astype(jnp.float32)
    columns = []
    for direction in range(3):
        spatial_axis = 4 - direction
        link_field = link_block[direction].reshape((2, 3, 3, depth_cells, side_cells, side_cells)).astype(jnp.float32)
        forward_field = jnp.roll(vectors_wide, -1, axis=spatial_axis)
        adjoint = times_adjoint(link_field, vectors_wide).astype(jnp.bfloat16)
        behind = lax.optimization_barrier(jnp.roll(adjoint, 1, axis=spatial_axis)).astype(jnp.float32)
        derived = (times_links(link_field, forward_field) - behind).astype(jnp.bfloat16)
        columns.append(derived.reshape((-1, mode_count)))
        columns.append(jnp.concatenate([derived[1], -derived[0]], axis=0).reshape((-1, mode_count)))
    stacked = jnp.stack(columns, axis=1).reshape((columns[0].shape[0], -1))
    flat_vectors = vectors.reshape((-1, mode_count))
    partial_sum = lax.dot_general(flat_vectors, stacked, (((0,), (0,)), ((), ())), preferred_element_type=jnp.float32)
    return (partial_sum * norm_scale).reshape((mode_count, 3, 2, mode_count))

def reference(eigenvectors, gauge_links, perambulators, source_times, insert_offsets, derivative_dirs):
    norm_scale = 1.0 / math.sqrt(24.0 * DEPTH * SIDE * SIDE)

    def first_section(inputs):
        vectors, link_block, peram_rows = inputs
        elementals = slice_elementals(vectors, link_block, norm_scale)
        rounded = lax.optimization_barrier(elementals.astype(jnp.bfloat16)).astype(jnp.float32)
        operator = operator_matrix(rounded, derivative_dirs)
        first_product = jnp.dot(peram_rows, operator, preferred_element_type=jnp.float32) * (1.0 / math.sqrt(ORDER))
        return (elementals, first_product.astype(jnp.bfloat16), trace_pair(first_product))
    elementals, first_rounded, first_traces = lax.map(first_section, (eigenvectors, gauge_links, perambulators))

    def next_section(inputs):
        left_rows, right_rows = inputs
        product = jnp.dot(left_rows, row_block(right_rows), preferred_element_type=jnp.float32)
        return (product.astype(jnp.bfloat16), product, trace_pair(product))
    second_rounded, second_product, second_traces = lax.map(next_section, (jnp.roll(first_rounded, -1, axis=0), first_rounded))
    third_rounded, third_product, third_traces = lax.map(next_section, (jnp.roll(second_rounded, -1, axis=0), first_rounded))
    chain_products = (third_product * math.sqrt(ORDER)).astype(jnp.bfloat16)
    traces = jnp.stack([first_traces, second_traces, third_traces], axis=1)
    correlator = correlate(traces, source_times, insert_offsets)
    return (elementals, chain_products, correlator)
```

```python
import functools
import math

import jax
import jax.numpy as jnp
import numpy as np
from jax import lax
from jax.experimental import pallas as pl
from jax.experimental.pallas import tpu as pltpu
from jax.sharding import PartitionSpec as P

MESH = pl.DeviceIdType.MESH
F32 = jnp.float32
BF16 = jnp.bfloat16
CHUNKS = 2


def dot(a, b, dims=(((1,), (0,)), ((), ()))):
    return lax.dot_general(a, b, dims, preferred_element_type=F32)


def shift_table(depth, side):
    site = np.arange(depth * side * side)
    z, y, x = site // (side * side), (site // side) % side, site % side
    targets = [
        (z * side + y) * side + (x + 1) % side,
        (z * side + (y + 1) % side) * side + x,
        (((z + 1) % depth) * side + y) * side + x,
    ]
    table = np.zeros((3 * site.size, site.size), np.float32)
    for direction, target in enumerate(targets):
        table[direction * site.size + site, target] = 1.0
    return table


def diagonal_sums(product, first_row):
    rows, width = product.shape
    order = width // 2
    hit = lax.broadcasted_iota(jnp.int32, (rows, order), 1) == (
        first_row + lax.broadcasted_iota(jnp.int32, (rows, order), 0)
    )
    return (
        jnp.sum(jnp.where(hit, product[:, :order], 0.0)),
        jnp.sum(jnp.where(hit, product[:, order:], 0.0)),
    )


def complex_rows(left, right):
    rows, width = left.shape
    order = width // 2
    both = dot(jnp.concatenate([left[:, :order], left[:, order:]], axis=0), right)
    top, bottom = both[:rows], both[rows:]
    return jnp.concatenate(
        [top[:, :order] - bottom[:, order:], top[:, order:] + bottom[:, :order]], axis=1
    )


def first_rows(peram, mixed):
    rows, width = peram.shape
    order = width // 2
    half = order // 2
    stacked = jnp.concatenate(
        [
            peram[:, half:order],
            peram[:, order + half :],
            peram[:, :half],
            peram[:, order : order + half],
        ],
        axis=0,
    )
    y = dot(stacked, mixed)
    down_real = y[:rows, :half] - y[rows : 2 * rows, half:]
    down_imag = y[:rows, half:] + y[rows : 2 * rows, :half]
    up_real = y[2 * rows : 3 * rows, :half] - y[3 * rows :, half:]
    up_imag = y[2 * rows : 3 * rows, half:] + y[3 * rows :, :half]
    return jnp.concatenate([-down_imag, up_imag, down_real, -up_real], axis=1) * (
        1.0 / math.sqrt(order)
    )


def kernel(
    sizes,
    v_ref,
    l_ref,
    p_ref,
    table_ref,
    src_ref,
    off_ref,
    dirs_ref,
    elem_ref,
    chain_ref,
    corr_ref,
    v_all,
    l_all,
    p_all,
    e_all,
    m_ref,
    f_all,
    f_next,
    s_own,
    s_next,
    t_all,
    v_send,
    v_recv,
    l_send,
    l_recv,
    p_send,
    p_recv,
    q_send,
    q_recv,
    z_send,
    z_recv,
    t_send,
    t_recv,
):
    T, S, K = sizes
    G = S * K
    t, s, k = lax.axis_index("tm"), lax.axis_index("space"), lax.axis_index("spin")
    rank = s * K + k
    rows = p_ref.shape[0]
    order = p_ref.shape[1] // 2
    modes = v_ref.shape[2]
    first_row = rank * rows
    mine = pl.ds(pl.multiple_of(first_row, rows), rows)
    below, above = lax.rem(t + T - 1, T), lax.rem(t + 1, T)

    barrier = pltpu.get_barrier_semaphore()
    for j in range(1, G):
        other = lax.rem(rank + j, G)
        pl.semaphore_signal(
            barrier,
            inc=1,
            device_id={"tm": t, "space": lax.div(other, K), "spin": lax.rem(other, K)},
            device_id_type=MESH,
        )
    for target in (below, above):
        pl.semaphore_signal(barrier, inc=1, device_id={"tm": target}, device_id_type=MESH)
    pl.semaphore_wait(barrier, G + 1)

    sends = []
    for j in range(1, S):
        other = lax.rem(s + j, S)
        for source, target, send_sem, recv_sem in (
            (v_ref, v_all.at[s], v_send, v_recv),
            (l_ref, l_all.at[s], l_send, l_recv),
        ):
            copy = pltpu.make_async_remote_copy(
                source, target, send_sem.at[j], recv_sem.at[s],
                device_id={"space": other}, device_id_type=MESH,
            )
            copy.start()
            sends.append(copy)
    for j in range(1, S):
        other = lax.rem(s + j, S)
        copy = pltpu.make_async_remote_copy(
            p_ref, p_all.at[mine], p_send.at[j], p_recv.at[s],
            device_id={"space": other}, device_id_type=MESH,
        )
        copy.start()
        sends.append(copy)
    for i in range(1, K):
        copy = pltpu.make_async_remote_copy(
            p_ref, p_all.at[mine], q_send.at[0, i], q_recv.at[rank],
            device_id={"spin": lax.rem(k + i, K)}, device_id_type=MESH,
        )
        copy.start()
        sends.append(copy)
    v_all[s] = v_ref[...]
    l_all[s] = l_ref[...]

    for j in range(1, S):
        other = lax.rem(s + j, S)
        for ref, sem in ((v_all, v_recv), (l_all, l_recv)):
            pltpu.make_async_copy(ref.at[other], ref.at[other], sem.at[other]).wait()

    slab = v_ref.shape[1]
    sites = S * slab
    fields = [jnp.concatenate([v_all[i, j] for i in range(S)], axis=0) for j in range(6)]
    moved = dot(table_ref[...], jnp.concatenate(fields, axis=1))
    eye = (
        lax.broadcasted_iota(jnp.int32, (slab, slab), 0)
        == lax.broadcasted_iota(jnp.int32, (slab, slab), 1)
    ).astype(F32).astype(BF16)
    links = jnp.concatenate(
        [dot(eye, l_all[i], (((1,), (1,)), ((), ()))) for i in range(S)], axis=0
    )
    columns = []
    for mu in range(3):
        ahead = [
            moved[mu * sites : (mu + 1) * sites, j * modes : (j + 1) * modes] for j in range(6)
        ]
        real_rows, imag_rows = [], []
        for c in range(3):
            real, imag = None, None
            for d in range(3):
                at = (mu * 6 + c) * 3 + d
                u_real = links[:, at : at + 1]
                u_imag = links[:, at + 9 : at + 10]
                more_real = u_real * ahead[d] - u_imag * ahead[3 + d]
                more_imag = u_real * ahead[3 + d] + u_imag * ahead[d]
                real = more_real if real is None else real + more_real
                imag = more_imag if imag is None else imag + more_imag
            real_rows.append(real.astype(BF16))
            imag_rows.append(imag.astype(BF16))
        columns.append(jnp.concatenate(real_rows + imag_rows, axis=0))
        columns.append(jnp.concatenate(imag_rows + [-r for r in real_rows], axis=0))
    norm_scale = 1.0 / math.sqrt(24.0 * sites)
    product = dot(
        jnp.concatenate(fields, axis=0), jnp.concatenate(columns, axis=1), (((0,), (0,)), ((), ()))
    ) * norm_scale
    for mu in range(3):
        a_real = product[:, (2 * mu) * modes : (2 * mu + 1) * modes]
        a_imag = product[:, (2 * mu + 1) * modes : (2 * mu + 2) * modes]
        e_all[mu, 0] = a_real - a_real.T
        e_all[mu, 1] = a_imag + a_imag.T

    def picked(gamma, part):
        return e_all[dirs_ref[gamma], part].astype(BF16).astype(F32)

    e0r, e0i, e1r, e1i, e2r, e2i = [picked(g, part) for g in range(3) for part in range(2)]
    m_ref[...] = jnp.concatenate(
        [
            jnp.concatenate([e2r, e0r + e1i, e2i, e0i - e1r], axis=1),
            jnp.concatenate([e0r - e1i, -e2r, e0i + e1r, -e2i], axis=1),
        ],
        axis=0,
    ).astype(BF16)

    part = rows // CHUNKS
    diagonals = []

    def to_below(source, target, index):
        copy = pltpu.make_async_remote_copy(
            source, target, z_send.at[index], z_recv.at[index],
            device_id={"tm": below}, device_id_type=MESH,
        )
        copy.start()
        return copy

    z_copies = []
    real_sum, imag_sum = 0.0, 0.0
    for i in range(CHUNKS):
        wide = first_rows(p_ref[i * part : (i + 1) * part, :], m_ref[...])
        span = pl.ds(pl.multiple_of(first_row + i * part, part), part)
        f_all[span, :] = wide.astype(BF16)
        z_copies.append(to_below(f_all.at[span], f_next.at[pl.ds(i * part, part)], i))
        more_real, more_imag = diagonal_sums(wide, first_row + i * part)
        real_sum, imag_sum = real_sum + more_real, imag_sum + more_imag
    diagonals += [real_sum, imag_sum]

    for j in range(1, S):
        other = lax.rem(s + j, S)
        block = pl.ds(pl.multiple_of((other * K + k) * rows, rows), rows)
        pltpu.make_async_copy(p_all.at[block], p_all.at[block], p_recv.at[other]).wait()
        for i in range(1, K):
            copy = pltpu.make_async_remote_copy(
                p_all.at[block], p_all.at[block], q_send.at[j, i], q_recv.at[other * K + k],
                device_id={"spin": lax.rem(k + i, K)}, device_id_type=MESH,
            )
            copy.start()
            sends.append(copy)
        f_all[block, :] = first_rows(p_all[block, :], m_ref[...]).astype(BF16)
    for j in range(S):
        for i in range(1, K):
            owner = lax.rem(s + j, S) * K + lax.rem(k + i, K)
            block = pl.ds(pl.multiple_of(owner * rows, rows), rows)
            pltpu.make_async_copy(p_all.at[block], p_all.at[block], q_recv.at[owner]).wait()
            f_all[block, :] = first_rows(p_all[block, :], m_ref[...]).astype(BF16)

    share, half = elem_ref.shape[0], elem_ref.shape[3]
    own_rows = pl.ds(pl.multiple_of(s * share, share), share)
    for mu in range(3):
        for ri in range(2):
            block = e_all[mu, ri, own_rows, :]
            mine_columns = block[:, :half]
            for i in range(1, K):
                mine_columns = jnp.where(k == i, block[:, i * half : (i + 1) * half], mine_columns)
            elem_ref[:, mu, ri, :] = mine_columns

    real_sum, imag_sum = 0.0, 0.0
    for i in range(CHUNKS):
        span = pl.ds(i * part, part)
        z_copies[i].wait_recv()
        wide = complex_rows(f_next[span, :], f_all[...])
        s_own[span, :] = wide.astype(BF16)
        z_copies.append(to_below(s_own.at[span], s_next.at[span], CHUNKS + i))
        more_real, more_imag = diagonal_sums(wide, first_row + i * part)
        real_sum, imag_sum = real_sum + more_real, imag_sum + more_imag
    diagonals += [real_sum, imag_sum]

    real_sum, imag_sum = 0.0, 0.0
    for i in range(CHUNKS):
        span = pl.ds(i * part, part)
        z_copies[CHUNKS + i].wait_recv()
        wide = complex_rows(s_next[span, :], f_all[...])
        chain_ref[span, :] = (wide * math.sqrt(order)).astype(BF16)
        more_real, more_imag = diagonal_sums(wide, first_row + i * part)
        real_sum, imag_sum = real_sum + more_real, imag_sum + more_imag
    diagonals += [real_sum, imag_sum]

    tile_row = lax.broadcasted_iota(jnp.int32, (8, 128), 0)
    tile_lane = lax.broadcasted_iota(jnp.int32, (8, 128), 1)
    tile = jnp.zeros((8, 128), F32)
    for o in range(3):
        for ri in range(2):
            tile = jnp.where((tile_row == o) & (tile_lane == ri), diagonals[2 * o + ri], tile)
    total = T * G
    me = t * G + rank
    t_all[me] = tile

    def trace_copy(j):
        other = lax.rem(me + j, total)
        group = lax.rem(other, G)
        return other, pltpu.make_async_remote_copy(
            t_all.at[me], t_all.at[me], t_send.at[j], t_recv.at[me],
            device_id={
                "tm": lax.div(other, G), "space": lax.div(group, K), "spin": lax.rem(group, K)
            },
            device_id_type=MESH,
        )

    def start_trace(j, carry):
        trace_copy(j)[1].start()
        return carry

    lax.fori_loop(1, total, start_trace, 0)

    def wait_trace(j, carry):
        other, copy = trace_copy(j)
        copy.wait_send()
        pltpu.make_async_copy(t_all.at[other], t_all.at[other], t_recv.at[other]).wait()
        return carry

    lax.fori_loop(1, total, wait_trace, 0)

    counts = []
    for o in range(3):
        count = 0
        for j in range(off_ref.shape[0]):
            count = count + jnp.where(off_ref[j] == o, 1, 0)
        counts.append(count.astype(F32))
    weight = jnp.zeros((8, 128), F32)
    for o in range(3):
        weight = jnp.where(tile_row == o, counts[o], weight)
    sources = src_ref.shape[0]
    out_row = lax.broadcasted_iota(jnp.int32, (sources, 128), 0)
    wanted = jnp.zeros((sources, 128), jnp.int32)
    for n in range(sources):
        wanted = jnp.where(out_row == n, src_ref[n], wanted)

    def add_time(i, acc):
        summed = t_all[i * G]
        for g in range(1, G):
            summed = summed + t_all[i * G + g]
        line = jnp.sum(summed * weight, axis=0, keepdims=True)
        return acc + jnp.where(wanted == i, line, 0.0)

    found = lax.fori_loop(0, T, add_time, jnp.zeros((sources, 128), F32))
    corr_ref[...] = found[:, : corr_ref.shape[1]]

    for copy in sends:
        copy.wait_send()
    for copy in z_copies:
        copy.wait_send()


def on_device(
    sizes, eigenvectors, gauge_links, perambulators, source_times, insert_offsets, derivative_dirs
):
    T, S, K = sizes
    _, _, _, planes, side, _, modes = eigenvectors.shape
    slab = planes * side * side
    vectors = eigenvectors.reshape((6, slab, modes))
    links = gauge_links.reshape((54, slab))
    peram = perambulators[0]
    rows, width = peram.shape
    order = width // 2
    table = jnp.asarray(shift_table(planes * S, side), BF16)
    vmem = pl.BlockSpec(memory_space=pltpu.VMEM)
    smem = pl.BlockSpec(memory_space=pltpu.SMEM)
    dma = pltpu.SemaphoreType.DMA
    elementals, chain, correlator = pl.pallas_call(
        functools.partial(kernel, sizes),
        out_shape=(
            jax.ShapeDtypeStruct((modes // S, 3, 2, modes // K), F32),
            jax.ShapeDtypeStruct((rows, width), BF16),
            jax.ShapeDtypeStruct((source_times.shape[0], 2), F32),
        ),
        in_specs=[vmem, vmem, vmem, vmem, smem, smem, smem],
        out_specs=(vmem, vmem, vmem),
        scratch_shapes=[
            pltpu.VMEM((S, 6, slab, modes), BF16),
            pltpu.VMEM((S, 54, slab), BF16),
            pltpu.VMEM((order, width), BF16),
            pltpu.VMEM((3, 2, modes, modes), F32),
            pltpu.VMEM((2 * modes, 4 * modes), BF16),
            pltpu.VMEM((order, width), BF16),
            pltpu.VMEM((rows, width), BF16),
            pltpu.VMEM((rows, width), BF16),
            pltpu.VMEM((rows, width), BF16),
            pltpu.VMEM((T * S * K, 8, 128), F32),
            dma((S,)),
            dma((S,)),
            dma((S,)),
            dma((S,)),
            dma((S,)),
            dma((S,)),
            dma((S, K)),
            dma((S * K,)),
            dma((2 * CHUNKS,)),
            dma((2 * CHUNKS,)),
            dma((T * S * K,)),
            dma((T * S * K,)),
        ],
        compiler_params=pltpu.CompilerParams(collective_id=0, has_side_effects=True),
    )(vectors, links, peram, table, source_times, insert_offsets, derivative_dirs)
    return (elementals[None], chain[None], correlator)


def solution(mesh):
    sizes = (mesh.shape["tm"], mesh.shape["space"], mesh.shape["spin"])
    in_specs = (
        P(("cfg", "tm"), None, None, "space", None, None, None),
        P(("cfg", "tm"), None, None, None, None, "space", None),
        P(("cfg", "tm"), ("space", "spin"), None),
        P(),
        P(),
        P(),
    )
    out_specs = (
        P(("cfg", "tm"), "space", None, None, "spin"),
        P(("cfg", "tm"), ("space", "spin"), None),
        P("cfg", None),
    )
    return jax.shard_map(
        functools.partial(on_device, sizes),
        mesh=mesh,
        in_specs=in_specs,
        out_specs=out_specs,
        check_vma=False,
    )
```

```python
import functools
import math

import jax
import jax.numpy as jnp
import numpy as np
from jax import lax
from jax.experimental import pallas as pl
from jax.experimental.pallas import tpu as pltpu
from jax.sharding import PartitionSpec as P

MESH = pl.DeviceIdType.MESH
F32 = jnp.float32
BF16 = jnp.bfloat16
CHUNKS = 4


def dot(a, b, dims=(((1,), (0,)), ((), ()))):
    return lax.dot_general(a, b, dims, preferred_element_type=F32)


def shift_table(slabs, planes, side):
    depth, area = slabs * planes, side * side
    slab, cell, plane = np.meshgrid(
        np.arange(slabs), np.arange(area), np.arange(planes), indexing="ij"
    )
    z, y, x = (slab * planes + plane).ravel(), (cell // side).ravel(), (cell % side).ravel()
    count = z.size

    def plain(z, y, x):
        return ((z % depth) * side + y % side) * side + x % side

    def ordered(z, y, x):
        z = z % depth
        return ((z // planes) * area + (y % side) * side + x % side) * planes + z % planes

    targets = [
        plain(z, y, x), plain(z, y, x + 1), plain(z, y + 1, x), plain(z + 1, y, x),
        ordered(z, y, x - 1), ordered(z, y - 1, x), ordered(z - 1, y, x),
    ]
    table = np.zeros((len(targets) * count, count), np.float32)
    for block, target in enumerate(targets):
        table[block * count + np.arange(count), target] = 1.0
    return table


def diagonal_lines(product, first_row, lanes=128):
    rows, width = product.shape
    order = width // 2
    hit = lax.broadcasted_iota(jnp.int32, (rows, order), 1) == (
        first_row + lax.broadcasted_iota(jnp.int32, (rows, order), 0)
    )
    lines = []
    for half in (product[:, :order], product[:, order:]):
        kept = jnp.where(hit, half, 0.0)
        folded = sum(kept[:, i : i + lanes] for i in range(0, order, lanes))
        lines.append(jnp.sum(folded, axis=0, keepdims=True))
    return jnp.concatenate(lines, axis=0)


def complex_rows(left, right):
    rows, width = left.shape
    order = width // 2
    both = dot(jnp.concatenate([left[:, :order], left[:, order:]], axis=0), right)
    top, bottom = both[:rows], both[rows:]
    return jnp.concatenate(
        [top[:, :order] - bottom[:, order:], top[:, order:] + bottom[:, :order]], axis=1
    )


def first_rows(peram, mixed):
    rows, width = peram.shape
    order = width // 2
    half = order // 2
    stacked = jnp.concatenate(
        [
            peram[:, half:order],
            peram[:, order + half :],
            peram[:, :half],
            peram[:, order : order + half],
        ],
        axis=0,
    )
    y = dot(stacked, mixed)
    down_real = y[:rows, :half] - y[rows : 2 * rows, half:]
    down_imag = y[:rows, half:] + y[rows : 2 * rows, :half]
    up_real = y[2 * rows : 3 * rows, :half] - y[3 * rows :, half:]
    up_imag = y[2 * rows : 3 * rows, half:] + y[3 * rows :, :half]
    return jnp.concatenate([-down_imag, up_imag, down_real, -up_real], axis=1) * (
        1.0 / math.sqrt(order)
    )


def kernel(
    sizes,
    v_ref,
    l_ref,
    p_ref,
    table_ref,
    src_ref,
    off_ref,
    dirs_ref,
    elem_ref,
    chain_ref,
    corr_ref,
    v_all,
    l_own,
    l_all,
    p_all,
    e_all,
    m_ref,
    f_all,
    f_next,
    s_own,
    s_next,
    t_all,
    v_send,
    v_recv,
    l_send,
    l_recv,
    p_send,
    p_recv,
    q_send,
    q_recv,
    z_send,
    z_recv,
    t_send,
    t_recv,
):
    T, S, K = sizes
    G = S * K
    t, s, k = lax.axis_index("tm"), lax.axis_index("space"), lax.axis_index("spin")
    rank = s * K + k
    rows = p_ref.shape[0]
    order = p_ref.shape[1] // 2
    modes = v_ref.shape[2]
    first_row = rank * rows
    mine = pl.ds(pl.multiple_of(first_row, rows), rows)
    below, above = lax.rem(t + T - 1, T), lax.rem(t + 1, T)

    planes = l_ref.shape[1]
    eye = (
        lax.broadcasted_iota(jnp.int32, (planes, planes), 0)
        == lax.broadcasted_iota(jnp.int32, (planes, planes), 1)
    ).astype(F32).astype(BF16)
    l_own[...] = dot(eye, l_ref[...], (((1,), (1,)), ((), ()))).astype(BF16)

    barrier = pltpu.get_barrier_semaphore()
    for j in range(1, G):
        other = lax.rem(rank + j, G)
        pl.semaphore_signal(
            barrier,
            inc=1,
            device_id={"tm": t, "space": lax.div(other, K), "spin": lax.rem(other, K)},
            device_id_type=MESH,
        )
    for target in (below, above):
        pl.semaphore_signal(barrier, inc=1, device_id={"tm": target}, device_id_type=MESH)
    pl.semaphore_wait(barrier, G + 1)

    sends = []
    for j in range(1, S):
        other = lax.rem(s + j, S)
        for source, target, send_sem, recv_sem in (
            (v_ref, v_all.at[s], v_send, v_recv),
            (l_own, l_all.at[s], l_send, l_recv),
        ):
            copy = pltpu.make_async_remote_copy(
                source, target, send_sem.at[j], recv_sem.at[s],
                device_id={"space": other}, device_id_type=MESH,
            )
            copy.start()
            sends.append(copy)
    for j in range(1, S):
        other = lax.rem(s + j, S)
        copy = pltpu.make_async_remote_copy(
            p_ref, p_all.at[mine], p_send.at[j], p_recv.at[s],
            device_id={"space": other}, device_id_type=MESH,
        )
        copy.start()
        sends.append(copy)
    for i in range(1, K):
        copy = pltpu.make_async_remote_copy(
            p_ref, p_all.at[mine], q_send.at[0, i], q_recv.at[rank],
            device_id={"spin": lax.rem(k + i, K)}, device_id_type=MESH,
        )
        copy.start()
        sends.append(copy)
    v_all[s] = v_ref[...]
    l_all[s] = l_own[...]

    for j in range(1, S):
        other = lax.rem(s + j, S)
        for ref, sem in ((v_all, v_recv), (l_all, l_recv)):
            pltpu.make_async_copy(ref.at[other], ref.at[other], sem.at[other]).wait()

    slab = v_ref.shape[1]
    sites = S * slab
    cells = slab // planes
    fields = [jnp.concatenate([v_all[i, j] for i in range(S)], axis=0) for j in range(6)]
    moved = dot(table_ref[: 4 * sites, :], jnp.concatenate(fields, axis=1))

    def field(block, j):
        return moved[block * sites : (block + 1) * sites, j * modes : (j + 1) * modes]

    here = [field(0, j) for j in range(6)]
    link_lines = [l_all[i].astype(F32) for i in range(S)]

    def link(mu, ri, row, column):
        first = (((mu * 2 + ri) * 3 + row) * 3 + column) * cells
        return jnp.concatenate(
            [
                jnp.broadcast_to(line[:, first + cell : first + cell + 1], (planes, modes))
                for line in link_lines
                for cell in range(cells)
            ],
            axis=0,
        )

    columns = []
    for mu in range(3):
        ahead = [field(1 + mu, j) for j in range(6)]
        forward = [0.0] * 6
        adjoint = [0.0] * 6
        for row in range(3):
            for column in range(3):
                real, imag = link(mu, 0, row, column), link(mu, 1, row, column)
                forward[row] += real * ahead[column] - imag * ahead[3 + column]
                forward[3 + row] += real * ahead[3 + column] + imag * ahead[column]
                adjoint[column] += real * here[row] + imag * here[3 + row]
                adjoint[3 + column] += real * here[3 + row] - imag * here[row]
        behind = dot(
            table_ref[(4 + mu) * sites : (5 + mu) * sites, :],
            jnp.concatenate([a.astype(BF16) for a in adjoint], axis=1),
        )
        derived = [
            (forward[j] - behind[:, j * modes : (j + 1) * modes]).astype(BF16) for j in range(6)
        ]
        columns.append(jnp.concatenate(derived, axis=0))
        columns.append(jnp.concatenate(derived[3:] + [-d for d in derived[:3]], axis=0))
    norm_scale = 1.0 / math.sqrt(24.0 * sites)
    product = dot(
        jnp.concatenate([h.astype(BF16) for h in here], axis=0),
        jnp.concatenate(columns, axis=1),
        (((0,), (0,)), ((), ())),
    ) * norm_scale
    for mu in range(3):
        for ri in range(2):
            at = (2 * mu + ri) * modes
            e_all[mu, ri] = product[:, at : at + modes]

    def picked(gamma, part):
        return e_all[dirs_ref[gamma], part].astype(BF16).astype(F32)

    e0r, e0i, e1r, e1i, e2r, e2i = [picked(g, part) for g in range(3) for part in range(2)]
    m_ref[...] = jnp.concatenate(
        [
            jnp.concatenate([e2r, e0r + e1i, e2i, e0i - e1r], axis=1),
            jnp.concatenate([e0r - e1i, -e2r, e0i + e1r, -e2i], axis=1),
        ],
        axis=0,
    ).astype(BF16)

    part = rows // CHUNKS
    diagonals = []

    def to_below(source, target, index):
        copy = pltpu.make_async_remote_copy(
            source, target, z_send.at[index], z_recv.at[index],
            device_id={"tm": below}, device_id_type=MESH,
        )
        copy.start()
        return copy

    z_copies = []
    lines = 0.0
    for i in range(CHUNKS):
        wide = first_rows(p_ref[i * part : (i + 1) * part, :], m_ref[...])
        span = pl.ds(pl.multiple_of(first_row + i * part, part), part)
        f_all[span, :] = wide.astype(BF16)
        z_copies.append(to_below(f_all.at[span], f_next.at[pl.ds(i * part, part)], i))
        lines += diagonal_lines(wide, first_row + i * part)
    diagonals.append(lines)

    for j in range(1, S):
        other = lax.rem(s + j, S)
        block = pl.ds(pl.multiple_of((other * K + k) * rows, rows), rows)
        pltpu.make_async_copy(p_all.at[block], p_all.at[block], p_recv.at[other]).wait()
        for i in range(1, K):
            copy = pltpu.make_async_remote_copy(
                p_all.at[block], p_all.at[block], q_send.at[j, i], q_recv.at[other * K + k],
                device_id={"spin": lax.rem(k + i, K)}, device_id_type=MESH,
            )
            copy.start()
            sends.append(copy)
        f_all[block, :] = first_rows(p_all[block, :], m_ref[...]).astype(BF16)
    for j in range(S):
        for i in range(1, K):
            owner = lax.rem(s + j, S) * K + lax.rem(k + i, K)
            block = pl.ds(pl.multiple_of(owner * rows, rows), rows)
            pltpu.make_async_copy(p_all.at[block], p_all.at[block], q_recv.at[owner]).wait()
            f_all[block, :] = first_rows(p_all[block, :], m_ref[...]).astype(BF16)

    share, half = elem_ref.shape[0], elem_ref.shape[3]
    own_rows = pl.ds(pl.multiple_of(s * share, share), share)
    for mu in range(3):
        for ri in range(2):
            block = e_all[mu, ri, own_rows, :]
            mine_columns = block[:, :half]
            for i in range(1, K):
                mine_columns = jnp.where(k == i, block[:, i * half : (i + 1) * half], mine_columns)
            elem_ref[:, mu, ri, :] = mine_columns

    lane = lax.broadcasted_iota(jnp.int32, (2, 128), 1)
    wanted = jnp.full((2, 128), -1, jnp.int32)
    for n in range(src_ref.shape[0]):
        wanted = jnp.where(lane == n, src_ref[n], wanted)
    tile_row = lax.broadcasted_iota(jnp.int32, (8, 128), 0)
    weight = jnp.zeros((8, 128), F32)
    for o in range(3):
        count = sum(jnp.where(off_ref[j] == o, 1, 0) for j in range(off_ref.shape[0]))
        weight = jnp.where(lax.div(tile_row, 2) == o, count.astype(F32), weight)

    lines = 0.0
    for i in range(CHUNKS):
        span = pl.ds(i * part, part)
        z_copies[i].wait_recv()
        wide = complex_rows(f_next[span, :], f_all[...])
        s_own[span, :] = wide.astype(BF16)
        z_copies.append(to_below(s_own.at[span], s_next.at[span], CHUNKS + i))
        lines += diagonal_lines(wide, first_row + i * part)
    diagonals.append(lines)

    lines = 0.0
    for i in range(CHUNKS):
        span = pl.ds(i * part, part)
        z_copies[CHUNKS + i].wait_recv()
        wide = complex_rows(s_next[span, :], f_all[...])
        chain_ref[span, :] = (wide * math.sqrt(order)).astype(BF16)
        lines += diagonal_lines(wide, first_row + i * part)
    diagonals.append(lines)

    t_all[t * G + rank] = jnp.concatenate(diagonals + [jnp.zeros((2, 128), F32)], axis=0)
    total = T * G
    me = t * G + rank

    def trace_copy(j):
        other = lax.rem(me + j, total)
        group = lax.rem(other, G)
        return other, pltpu.make_async_remote_copy(
            t_all.at[me], t_all.at[me], t_send.at[j], t_recv.at[me],
            device_id={
                "tm": lax.div(other, G), "space": lax.div(group, K), "spin": lax.rem(group, K)
            },
            device_id_type=MESH,
        )

    def start_trace(j, carry):
        trace_copy(j)[1].start()
        return carry

    lax.fori_loop(1, total, start_trace, 0)

    def wait_trace(j, carry):
        other, copy = trace_copy(j)
        copy.wait_send()
        pltpu.make_async_copy(t_all.at[other], t_all.at[other], t_recv.at[other]).wait()
        return carry

    lax.fori_loop(1, total, wait_trace, 0)

    def add_time(i, acc):
        summed = t_all[i * G]
        for g in range(1, G):
            summed = summed + t_all[i * G + g]
        weighted = jnp.sum(summed * weight, axis=1, keepdims=True)
        pair = weighted[0:2] + weighted[2:4] + weighted[4:6]
        return acc + jnp.where(wanted == i, pair, 0.0)

    found = lax.fori_loop(0, T, add_time, jnp.zeros((2, 128), F32))
    corr_ref[...] = found[:, : corr_ref.shape[1]]

    for copy in sends:
        copy.wait_send()
    for copy in z_copies:
        copy.wait_send()


def copy_kernel(*refs):
    for source, target in zip(refs[:3], refs[3:]):
        target[...] = source[...]


def on_device(
    sizes, eigenvectors, gauge_links, perambulators, source_times, insert_offsets, derivative_dirs
):
    T, S, K = sizes
    _, _, _, planes, side, _, modes = eigenvectors.shape
    slab = planes * side * side
    vectors = eigenvectors.reshape((6, slab, modes))
    links = jnp.swapaxes(gauge_links, 5, 6).reshape((54 * side * side, planes))
    peram = perambulators[0]
    rows, width = peram.shape
    order = width // 2
    table = jnp.asarray(shift_table(S, planes, side), BF16)
    vmem = pl.BlockSpec(memory_space=pltpu.VMEM)
    smem = pl.BlockSpec(memory_space=pltpu.SMEM)
    dma = pltpu.SemaphoreType.DMA
    elementals, chain, correlator = pl.pallas_call(
        functools.partial(kernel, sizes),
        out_shape=(
            jax.ShapeDtypeStruct((modes // S, 3, 2, modes // K), F32),
            jax.ShapeDtypeStruct((rows, width), BF16),
            jax.ShapeDtypeStruct((2, source_times.shape[0]), F32),
        ),
        in_specs=[vmem, vmem, vmem, vmem, smem, smem, smem],
        out_specs=(vmem, vmem, vmem),
        scratch_shapes=[
            pltpu.VMEM((S, 6, slab, modes), BF16),
            pltpu.VMEM((planes, 54 * side * side), BF16),
            pltpu.VMEM((S, planes, 54 * side * side), BF16),
            pltpu.VMEM((order, width), BF16),
            pltpu.VMEM((3, 2, modes, modes), F32),
            pltpu.VMEM((2 * modes, 4 * modes), BF16),
            pltpu.VMEM((order, width), BF16),
            pltpu.VMEM((rows, width), BF16),
            pltpu.VMEM((rows, width), BF16),
            pltpu.VMEM((rows, width), BF16),
            pltpu.VMEM((T * S * K, 8, 128), F32),
            dma((S,)),
            dma((S,)),
            dma((S,)),
            dma((S,)),
            dma((S,)),
            dma((S,)),
            dma((S, K)),
            dma((S * K,)),
            dma((2 * CHUNKS,)),
            dma((2 * CHUNKS,)),
            dma((T * S * K,)),
            dma((T * S * K,)),
        ],
        compiler_params=pltpu.CompilerParams(collective_id=0, has_side_effects=True),
    )(vectors, links, peram, table, source_times, insert_offsets, derivative_dirs)
    elementals, chain, correlator = pl.pallas_call(
        copy_kernel,
        out_shape=tuple(jax.ShapeDtypeStruct(a.shape, a.dtype) for a in (elementals, chain, correlator)),
        in_specs=[vmem] * 3,
        out_specs=(vmem,) * 3,
    )(elementals, chain, correlator)
    return (elementals[None], chain[None], correlator.T)


def solution(mesh):
    sizes = (mesh.shape["tm"], mesh.shape["space"], mesh.shape["spin"])
    in_specs = (
        P(("cfg", "tm"), None, None, "space", None, None, None),
        P(("cfg", "tm"), None, None, None, None, "space", None),
        P(("cfg", "tm"), ("space", "spin"), None),
        P(),
        P(),
        P(),
    )
    out_specs = (
        P(("cfg", "tm"), "space", None, None, "spin"),
        P(("cfg", "tm"), ("space", "spin"), None),
        P("cfg", None),
    )
    return jax.shard_map(
        functools.partial(on_device, sizes),
        mesh=mesh,
        in_specs=in_specs,
        out_specs=out_specs,
        check_vma=False,
    )
```

```python
import functools
import math

import jax
import jax.numpy as jnp
import numpy as np
from jax import lax
from jax.experimental import pallas as pl
from jax.experimental.pallas import tpu as pltpu
from jax.sharding import PartitionSpec as P

MESH = pl.DeviceIdType.MESH
F32 = jnp.float32
BF16 = jnp.bfloat16
CHUNKS = 4
PIECES = 2


def dot(a, b, dims=(((1,), (0,)), ((), ()))):
    return lax.dot_general(a, b, dims, preferred_element_type=F32)


def shift_table(slabs, planes, side):
    depth, area = slabs * planes, side * side
    slab, cell, plane = np.meshgrid(
        np.arange(slabs), np.arange(area), np.arange(planes), indexing="ij"
    )
    z, y, x = (slab * planes + plane).ravel(), (cell // side).ravel(), (cell % side).ravel()
    count = z.size

    def plain(z, y, x):
        return ((z % depth) * side + y % side) * side + x % side

    def ordered(z, y, x):
        z = z % depth
        return ((z // planes) * area + (y % side) * side + x % side) * planes + z % planes

    targets = [
        plain(z, y, x), plain(z, y, x + 1), plain(z, y + 1, x), plain(z + 1, y, x),
        ordered(z, y, x - 1), ordered(z, y - 1, x), ordered(z - 1, y, x),
    ]
    table = np.zeros((len(targets) * count, count), np.float32)
    for block, target in enumerate(targets):
        table[block * count + np.arange(count), target] = 1.0
    return table


def diagonal_lines(product, first_row, lanes=128):
    rows, width = product.shape
    order = width // 2
    hit = lax.broadcasted_iota(jnp.int32, (rows, order), 1) == (
        first_row + lax.broadcasted_iota(jnp.int32, (rows, order), 0)
    )
    lines = []
    for half in (product[:, :order], product[:, order:]):
        kept = jnp.where(hit, half, 0.0)
        folded = sum(kept[:, i : i + lanes] for i in range(0, order, lanes))
        lines.append(jnp.sum(folded, axis=0, keepdims=True))
    return jnp.concatenate(lines, axis=0)


def complex_rows(left, right):
    rows, width = left.shape
    order = width // 2
    both = dot(jnp.concatenate([left[:, :order], left[:, order:]], axis=0), right)
    top, bottom = both[:rows], both[rows:]
    return jnp.concatenate(
        [top[:, :order] - bottom[:, order:], top[:, order:] + bottom[:, :order]], axis=1
    )


def first_rows(peram, mixed):
    rows, width = peram.shape
    order = width // 2
    half = order // 2
    stacked = jnp.concatenate(
        [
            peram[:, half:order],
            peram[:, order + half :],
            peram[:, :half],
            peram[:, order : order + half],
        ],
        axis=0,
    )
    y = dot(stacked, mixed)
    down_real = y[:rows, :half] - y[rows : 2 * rows, half:]
    down_imag = y[:rows, half:] + y[rows : 2 * rows, :half]
    up_real = y[2 * rows : 3 * rows, :half] - y[3 * rows :, half:]
    up_imag = y[2 * rows : 3 * rows, half:] + y[3 * rows :, :half]
    return jnp.concatenate([-down_imag, up_imag, down_real, -up_real], axis=1) * (
        1.0 / math.sqrt(order)
    )


def kernel(
    sizes,
    v_ref,
    l_ref,
    p_ref,
    table_ref,
    src_ref,
    off_ref,
    dirs_ref,
    elem_ref,
    chain_ref,
    corr_ref,
    l_in,
    table_in,
    in_sem,
    v_all,
    l_own,
    l_all,
    p_all,
    e_all,
    m_ref,
    f_all,
    f_next,
    s_own,
    s_next,
    t_all,
    v_send,
    v_recv,
    l_send,
    l_recv,
    p_send,
    p_recv,
    q_send,
    q_recv,
    z_send,
    z_recv,
    t_send,
    t_recv,
):
    T, S, K = sizes
    G = S * K
    t, s, k = lax.axis_index("tm"), lax.axis_index("space"), lax.axis_index("spin")
    rank = s * K + k
    rows = p_ref.shape[0]
    order = p_ref.shape[1] // 2
    modes = v_ref.shape[2]
    first_row = rank * rows
    mine = pl.ds(pl.multiple_of(first_row, rows), rows)
    below, above = lax.rem(t + T - 1, T), lax.rem(t + 1, T)

    loads = [
        pltpu.make_async_copy(source, target, in_sem.at[i])
        for i, (source, target) in enumerate(
            (
                (l_ref, l_in),
                (v_ref, v_all.at[s]),
                (p_ref, p_all.at[mine]),
                (table_ref, table_in),
            )
        )
    ]
    for load in loads:
        load.start()
    planes = l_ref.shape[1]
    barrier = pltpu.get_barrier_semaphore()
    for j in range(1, G):
        other = lax.rem(rank + j, G)
        pl.semaphore_signal(
            barrier,
            inc=1,
            device_id={"tm": t, "space": lax.div(other, K), "spin": lax.rem(other, K)},
            device_id_type=MESH,
        )
    for target in (below, above):
        pl.semaphore_signal(barrier, inc=1, device_id={"tm": target}, device_id_type=MESH)
    eye = (
        lax.broadcasted_iota(jnp.int32, (planes, planes), 0)
        == lax.broadcasted_iota(jnp.int32, (planes, planes), 1)
    ).astype(F32).astype(BF16)
    loads[0].wait()
    l_own[...] = dot(eye, l_in[...], (((1,), (1,)), ((), ()))).astype(BF16)
    for load in loads[1:]:
        load.wait()
    pl.semaphore_wait(barrier, G + 1)

    sends = []
    for j in range(1, S):
        other = lax.rem(s + j, S)
        for source, target, send_sem, recv_sem in (
            (v_all.at[s], v_all.at[s], v_send, v_recv),
            (l_own, l_all.at[s], l_send, l_recv),
        ):
            copy = pltpu.make_async_remote_copy(
                source, target, send_sem.at[j], recv_sem.at[s],
                device_id={"space": other}, device_id_type=MESH,
            )
            copy.start()
            sends.append(copy)
    piece = rows // PIECES

    def block_of(owner, c):
        return pl.ds(pl.multiple_of(owner * rows + c * piece, piece), piece)

    for c in range(PIECES):
        block = p_all.at[block_of(rank, c)]
        for j in range(1, S):
            copy = pltpu.make_async_remote_copy(
                block, block, p_send.at[j, c], p_recv.at[s, c],
                device_id={"space": lax.rem(s + j, S)}, device_id_type=MESH,
            )
            copy.start()
            sends.append(copy)
    for c in range(PIECES):
        block = p_all.at[block_of(rank, c)]
        for i in range(1, K):
            copy = pltpu.make_async_remote_copy(
                block, block, q_send.at[0, i, c], q_recv.at[rank, c],
                device_id={"spin": lax.rem(k + i, K)}, device_id_type=MESH,
            )
            copy.start()
            sends.append(copy)
    l_all[s] = l_own[...]

    for j in range(1, S):
        other = lax.rem(s + j, S)
        for ref, sem in ((v_all, v_recv), (l_all, l_recv)):
            pltpu.make_async_copy(ref.at[other], ref.at[other], sem.at[other]).wait()

    slab = v_ref.shape[1]
    sites = S * slab
    cells = slab // planes
    fields = [jnp.concatenate([v_all[i, j] for i in range(S)], axis=0) for j in range(6)]
    moved = dot(table_in[: 4 * sites, :], jnp.concatenate(fields, axis=1))

    def field(block, j):
        return moved[block * sites : (block + 1) * sites, j * modes : (j + 1) * modes]

    here = [field(0, j) for j in range(6)]
    link_lines = [l_all[i].astype(F32) for i in range(S)]

    def link(mu, ri, row, column):
        first = (((mu * 2 + ri) * 3 + row) * 3 + column) * cells
        return jnp.concatenate(
            [
                jnp.broadcast_to(line[:, first + cell : first + cell + 1], (planes, modes))
                for line in link_lines
                for cell in range(cells)
            ],
            axis=0,
        )

    columns = []
    for mu in range(3):
        ahead = [field(1 + mu, j) for j in range(6)]
        forward = [0.0] * 6
        adjoint = [0.0] * 6
        for row in range(3):
            for column in range(3):
                real, imag = link(mu, 0, row, column), link(mu, 1, row, column)
                forward[row] += real * ahead[column] - imag * ahead[3 + column]
                forward[3 + row] += real * ahead[3 + column] + imag * ahead[column]
                adjoint[column] += real * here[row] + imag * here[3 + row]
                adjoint[3 + column] += real * here[3 + row] - imag * here[row]
        behind = dot(
            table_in[(4 + mu) * sites : (5 + mu) * sites, :],
            jnp.concatenate([a.astype(BF16) for a in adjoint], axis=1),
        )
        derived = [
            (forward[j] - behind[:, j * modes : (j + 1) * modes]).astype(BF16) for j in range(6)
        ]
        columns.append(jnp.concatenate(derived, axis=0))
        columns.append(jnp.concatenate(derived[3:] + [-d for d in derived[:3]], axis=0))
    norm_scale = 1.0 / math.sqrt(24.0 * sites)
    product = dot(
        jnp.concatenate([h.astype(BF16) for h in here], axis=0),
        jnp.concatenate(columns, axis=1),
        (((0,), (0,)), ((), ())),
    ) * norm_scale
    for mu in range(3):
        for ri in range(2):
            at = (2 * mu + ri) * modes
            e_all[mu, ri] = product[:, at : at + modes]

    def picked(gamma, part):
        return e_all[dirs_ref[gamma], part].astype(BF16).astype(F32)

    e0r, e0i, e1r, e1i, e2r, e2i = [picked(g, part) for g in range(3) for part in range(2)]
    m_ref[...] = jnp.concatenate(
        [
            jnp.concatenate([e2r, e0r + e1i, e2i, e0i - e1r], axis=1),
            jnp.concatenate([e0r - e1i, -e2r, e0i + e1r, -e2i], axis=1),
        ],
        axis=0,
    ).astype(BF16)

    part = rows // CHUNKS
    diagonals = []

    def to_below(source, target, index):
        copy = pltpu.make_async_remote_copy(
            source, target, z_send.at[index], z_recv.at[index],
            device_id={"tm": below}, device_id_type=MESH,
        )
        copy.start()
        return copy

    z_copies = []
    lines = 0.0
    for i in range(CHUNKS):
        span = pl.ds(pl.multiple_of(first_row + i * part, part), part)
        wide = first_rows(p_all[span, :], m_ref[...])
        f_all[span, :] = wide.astype(BF16)
        z_copies.append(to_below(f_all.at[span], f_next.at[pl.ds(i * part, part)], i))
        lines += diagonal_lines(wide, first_row + i * part)
    diagonals.append(lines)

    def arrived(owner, c, sem):
        block = p_all.at[block_of(owner, c)]
        pltpu.make_async_copy(block, block, sem).wait()

    def multiply(owner, c):
        block = block_of(owner, c)
        f_all[block, :] = first_rows(p_all[block, :], m_ref[...]).astype(BF16)

    for i in range(1, K):
        owner = s * K + lax.rem(k + i, K)
        for c in range(PIECES):
            arrived(owner, c, q_recv.at[owner, c])
            multiply(owner, c)
    for c in range(PIECES):
        for j in range(1, S):
            other = lax.rem(s + j, S)
            owner = other * K + k
            arrived(owner, c, p_recv.at[other, c])
            for i in range(1, K):
                block = p_all.at[block_of(owner, c)]
                copy = pltpu.make_async_remote_copy(
                    block, block, q_send.at[j, i, c], q_recv.at[owner, c],
                    device_id={"spin": lax.rem(k + i, K)}, device_id_type=MESH,
                )
                copy.start()
                sends.append(copy)
            multiply(owner, c)
        for j in range(1, S):
            for i in range(1, K):
                owner = lax.rem(s + j, S) * K + lax.rem(k + i, K)
                arrived(owner, c, q_recv.at[owner, c])
                multiply(owner, c)

    lane = lax.broadcasted_iota(jnp.int32, (2, 128), 1)
    wanted = jnp.full((2, 128), -1, jnp.int32)
    for n in range(src_ref.shape[0]):
        wanted = jnp.where(lane == n, src_ref[n], wanted)
    tile_row = lax.broadcasted_iota(jnp.int32, (8, 128), 0)
    weight = jnp.zeros((8, 128), F32)
    for o in range(3):
        count = sum(jnp.where(off_ref[j] == o, 1, 0) for j in range(off_ref.shape[0]))
        weight = jnp.where(lax.div(tile_row, 2) == o, count.astype(F32), weight)

    lines = 0.0
    for i in range(CHUNKS):
        span = pl.ds(i * part, part)
        z_copies[i].wait_recv()
        wide = complex_rows(f_next[span, :], f_all[...])
        s_own[span, :] = wide.astype(BF16)
        z_copies.append(to_below(s_own.at[span], s_next.at[span], CHUNKS + i))
        lines += diagonal_lines(wide, first_row + i * part)
    diagonals.append(lines)

    share, half = elem_ref.shape[0], elem_ref.shape[3]
    own_rows = pl.ds(pl.multiple_of(s * share, share), share)
    for mu in range(3):
        for ri in range(2):
            block = e_all[mu, ri, own_rows, :]
            mine_columns = block[:, :half]
            for i in range(1, K):
                mine_columns = jnp.where(k == i, block[:, i * half : (i + 1) * half], mine_columns)
            elem_ref[:, mu, ri, :] = mine_columns

    lines = 0.0
    for i in range(CHUNKS):
        span = pl.ds(i * part, part)
        z_copies[CHUNKS + i].wait_recv()
        wide = complex_rows(s_next[span, :], f_all[...])
        chain_ref[span, :] = (wide * math.sqrt(order)).astype(BF16)
        lines += diagonal_lines(wide, first_row + i * part)
    diagonals.append(lines)

    t_all[t * G + rank] = jnp.concatenate(diagonals + [jnp.zeros((2, 128), F32)], axis=0)
    total = T * G
    me = t * G + rank

    def trace_copy(j):
        other = lax.rem(me + j, total)
        group = lax.rem(other, G)
        return other, pltpu.make_async_remote_copy(
            t_all.at[me], t_all.at[me], t_send.at[j], t_recv.at[me],
            device_id={
                "tm": lax.div(other, G), "space": lax.div(group, K), "spin": lax.rem(group, K)
            },
            device_id_type=MESH,
        )

    def start_trace(j, carry):
        trace_copy(j)[1].start()
        return carry

    lax.fori_loop(1, total, start_trace, 0)

    def wait_trace(j, carry):
        other, copy = trace_copy(j)
        copy.wait_send()
        pltpu.make_async_copy(t_all.at[other], t_all.at[other], t_recv.at[other]).wait()
        return carry

    lax.fori_loop(1, total, wait_trace, 0)

    def add_time(i, acc):
        summed = t_all[i * G]
        for g in range(1, G):
            summed = summed + t_all[i * G + g]
        weighted = jnp.sum(summed * weight, axis=1, keepdims=True)
        pair = weighted[0:2] + weighted[2:4] + weighted[4:6]
        return acc + jnp.where(wanted == i, pair, 0.0)

    found = lax.fori_loop(0, T, add_time, jnp.zeros((2, 128), F32))
    corr_ref[...] = found[:, : corr_ref.shape[1]]

    for copy in sends:
        copy.wait_send()
    for copy in z_copies:
        copy.wait_send()


def copy_kernel(*refs):
    copies = [
        pltpu.make_async_copy(refs[i], refs[3 + i], refs[6].at[i]) for i in range(3)
    ]
    for copy in copies:
        copy.start()
    for copy in copies:
        copy.wait()


def on_device(
    sizes, eigenvectors, gauge_links, perambulators, source_times, insert_offsets, derivative_dirs
):
    T, S, K = sizes
    _, _, _, planes, side, _, modes = eigenvectors.shape
    slab = planes * side * side
    vectors = eigenvectors.reshape((6, slab, modes))
    links = jnp.swapaxes(gauge_links, 5, 6).reshape((54 * side * side, planes))
    peram = perambulators[0]
    rows, width = peram.shape
    order = width // 2
    table = jnp.asarray(shift_table(S, planes, side), BF16)
    vmem = pl.BlockSpec(memory_space=pltpu.VMEM)
    hbm = pl.BlockSpec(memory_space=pltpu.HBM)
    smem = pl.BlockSpec(memory_space=pltpu.SMEM)
    dma = pltpu.SemaphoreType.DMA
    elementals, chain, correlator = pl.pallas_call(
        functools.partial(kernel, sizes),
        out_shape=(
            pltpu.VMEM((modes // S, 3, 2, modes // K), F32),
            pltpu.VMEM((rows, width), BF16),
            pltpu.VMEM((2, source_times.shape[0]), F32),
        ),
        in_specs=[hbm, hbm, hbm, hbm, smem, smem, smem],
        out_specs=(vmem, vmem, vmem),
        scratch_shapes=[
            pltpu.VMEM(links.shape, BF16),
            pltpu.VMEM(table.shape, BF16),
            dma((4,)),
            pltpu.VMEM((S, 6, slab, modes), BF16),
            pltpu.VMEM((planes, 54 * side * side), BF16),
            pltpu.VMEM((S, planes, 54 * side * side), BF16),
            pltpu.VMEM((order, width), BF16),
            pltpu.VMEM((3, 2, modes, modes), F32),
            pltpu.VMEM((2 * modes, 4 * modes), BF16),
            pltpu.VMEM((order, width), BF16),
            pltpu.VMEM((rows, width), BF16),
            pltpu.VMEM((rows, width), BF16),
            pltpu.VMEM((rows, width), BF16),
            pltpu.VMEM((T * S * K, 8, 128), F32),
            dma((S,)),
            dma((S,)),
            dma((S,)),
            dma((S,)),
            dma((S, PIECES)),
            dma((S, PIECES)),
            dma((S, K, PIECES)),
            dma((S * K, PIECES)),
            dma((2 * CHUNKS,)),
            dma((2 * CHUNKS,)),
            dma((T * S * K,)),
            dma((T * S * K,)),
        ],
        compiler_params=pltpu.CompilerParams(collective_id=0, has_side_effects=True),
    )(vectors, links, peram, table, source_times, insert_offsets, derivative_dirs)
    elementals, chain, correlator = pl.pallas_call(
        copy_kernel,
        out_shape=tuple(jax.ShapeDtypeStruct(a.shape, a.dtype) for a in (elementals, chain, correlator)),
        in_specs=[vmem] * 3,
        out_specs=(pl.BlockSpec(memory_space=pl.ANY),) * 3,
        scratch_shapes=[dma((3,))],
    )(*(pltpu.with_memory_space_constraint(a, pltpu.VMEM) for a in (elementals, chain, correlator)))
    return (elementals[None], chain[None], correlator.T)


def solution(mesh):
    sizes = (mesh.shape["tm"], mesh.shape["space"], mesh.shape["spin"])
    in_specs = (
        P(("cfg", "tm"), None, None, "space", None, None, None),
        P(("cfg", "tm"), None, None, None, None, "space", None),
        P(("cfg", "tm"), ("space", "spin"), None),
        P(),
        P(),
        P(),
    )
    out_specs = (
        P(("cfg", "tm"), "space", None, None, "spin"),
        P(("cfg", "tm"), ("space", "spin"), None),
        P("cfg", None),
    )
    return jax.shard_map(
        functools.partial(on_device, sizes),
        mesh=mesh,
        in_specs=in_specs,
        out_specs=out_specs,
        check_vma=False,
    )
```

```python
import functools
import math

import jax
import jax.numpy as jnp
import numpy as np
from jax import lax
from jax.experimental import pallas as pl
from jax.experimental.pallas import tpu as pltpu
from jax.sharding import PartitionSpec as P

MESH = pl.DeviceIdType.MESH
F32 = jnp.float32
BF16 = jnp.bfloat16
CHUNK_ROWS = 16
PIECES = 2


def dot(a, b, dims=(((1,), (0,)), ((), ()))):
    return lax.dot_general(a, b, dims, preferred_element_type=F32)


def shift_table(slabs, planes, side):
    depth, area = slabs * planes, side * side
    slab, cell, plane = np.meshgrid(
        np.arange(slabs), np.arange(area), np.arange(planes), indexing="ij"
    )
    z, y, x = (slab * planes + plane).ravel(), (cell // side).ravel(), (cell % side).ravel()
    count = z.size

    def plain(z, y, x):
        return ((z % depth) * side + y % side) * side + x % side

    def ordered(z, y, x):
        z = z % depth
        return ((z // planes) * area + (y % side) * side + x % side) * planes + z % planes

    targets = [
        plain(z, y, x), plain(z, y, x + 1), plain(z, y + 1, x), plain(z + 1, y, x),
        ordered(z, y, x - 1), ordered(z, y - 1, x), ordered(z - 1, y, x),
    ]
    table = np.zeros((len(targets) * count, count), np.float32)
    for block, target in enumerate(targets):
        table[block * count + np.arange(count), target] = 1.0
    return table


def diagonal_lines(product, first_row, lanes=128):
    rows, width = product.shape
    order = width // 2
    hit = lax.broadcasted_iota(jnp.int32, (rows, order), 1) == (
        first_row + lax.broadcasted_iota(jnp.int32, (rows, order), 0)
    )
    lines = []
    for half in (product[:, :order], product[:, order:]):
        kept = jnp.where(hit, half, 0.0)
        folded = sum(kept[:, i : i + lanes] for i in range(0, order, lanes))
        lines.append(jnp.sum(folded, axis=0, keepdims=True))
    return jnp.concatenate(lines, axis=0)


def complex_rows(left, right):
    rows, width = left.shape
    order = width // 2
    both = dot(jnp.concatenate([left[:, :order], left[:, order:]], axis=0), right)
    top, bottom = both[:rows], both[rows:]
    return jnp.concatenate(
        [top[:, :order] - bottom[:, order:], top[:, order:] + bottom[:, :order]], axis=1
    )


def first_rows(peram, mixed):
    rows, width = peram.shape
    order = width // 2
    half = order // 2
    stacked = jnp.concatenate(
        [
            peram[:, half:order],
            peram[:, order + half :],
            peram[:, :half],
            peram[:, order : order + half],
        ],
        axis=0,
    )
    y = dot(stacked, mixed)
    down_real = y[:rows, :half] - y[rows : 2 * rows, half:]
    down_imag = y[:rows, half:] + y[rows : 2 * rows, :half]
    up_real = y[2 * rows : 3 * rows, :half] - y[3 * rows :, half:]
    up_imag = y[2 * rows : 3 * rows, half:] + y[3 * rows :, :half]
    return jnp.concatenate([-down_imag, up_imag, down_real, -up_real], axis=1) * (
        1.0 / math.sqrt(order)
    )


def kernel(
    sizes,
    v_ref,
    l_ref,
    p_ref,
    table_ref,
    src_ref,
    off_ref,
    dirs_ref,
    elem_ref,
    chain_ref,
    corr_ref,
    l_in,
    table_in,
    in_sem,
    v_all,
    l_own,
    l_all,
    p_all,
    e_all,
    m_ref,
    f_all,
    f_next,
    s_own,
    s_next,
    t_all,
    v_send,
    v_recv,
    l_send,
    l_recv,
    p_send,
    p_recv,
    q_send,
    q_recv,
    ready,
    z_send,
    z_recv,
    t_send,
    t_recv,
):
    T, S, K = sizes
    G = S * K
    t, s, k = lax.axis_index("tm"), lax.axis_index("space"), lax.axis_index("spin")
    rank = s * K + k
    rows = p_ref.shape[0]
    order = p_ref.shape[1] // 2
    modes = v_ref.shape[2]
    first_row = rank * rows
    mine = pl.ds(pl.multiple_of(first_row, rows), rows)
    below, above = lax.rem(t + T - 1, T), lax.rem(t + 1, T)

    loads = [
        pltpu.make_async_copy(source, target, in_sem.at[i])
        for i, (source, target) in enumerate(
            (
                (l_ref, l_in),
                (v_ref, v_all.at[s]),
                (p_ref, p_all.at[mine]),
                (table_ref, table_in),
            )
        )
    ]
    for load in loads:
        load.start()
    planes = l_ref.shape[1]
    barrier = pltpu.get_barrier_semaphore()
    for j in range(1, G):
        other = lax.rem(rank + j, G)
        pl.semaphore_signal(
            barrier,
            inc=1,
            device_id={"tm": t, "space": lax.div(other, K), "spin": lax.rem(other, K)},
            device_id_type=MESH,
        )
    pl.semaphore_signal(barrier, inc=1, device_id={"tm": below}, device_id_type=MESH)
    entered = G
    if T > 4:
        def announce(j, carry):
            other = lax.rem(t * G + rank + j, T * G)
            group = lax.rem(other, G)
            pl.semaphore_signal(
                barrier,
                inc=1,
                device_id={
                    "tm": lax.div(other, G), "space": lax.div(group, K), "spin": lax.rem(group, K)
                },
                device_id_type=MESH,
            )
            return carry

        lax.fori_loop(1, T * G, announce, 0)
        entered += T * G - 1
    eye = (
        lax.broadcasted_iota(jnp.int32, (planes, planes), 0)
        == lax.broadcasted_iota(jnp.int32, (planes, planes), 1)
    ).astype(F32).astype(BF16)
    loads[0].wait()
    l_own[...] = dot(eye, l_in[...], (((1,), (1,)), ((), ()))).astype(BF16)
    for load in loads[1:]:
        load.wait()
    pl.semaphore_wait(barrier, entered)
    pl.semaphore_signal(ready, inc=1, device_id={"tm": above}, device_id_type=MESH)

    sends = []
    for j in range(1, S):
        other = lax.rem(s + j, S)
        for source, target, send_sem, recv_sem in (
            (v_all.at[s], v_all.at[s], v_send, v_recv),
            (l_own, l_all.at[s], l_send, l_recv),
        ):
            copy = pltpu.make_async_remote_copy(
                source, target, send_sem.at[j], recv_sem.at[s],
                device_id={"space": other}, device_id_type=MESH,
            )
            copy.start()
            sends.append(copy)
    piece = rows // PIECES

    def block_of(owner, c):
        return pl.ds(pl.multiple_of(owner * rows + c * piece, piece), piece)

    for c in range(PIECES):
        block = p_all.at[block_of(rank, c)]
        for j in range(1, S):
            copy = pltpu.make_async_remote_copy(
                block, block, p_send.at[j, c], p_recv.at[s, c],
                device_id={"space": lax.rem(s + j, S)}, device_id_type=MESH,
            )
            copy.start()
            sends.append(copy)
    for c in range(PIECES):
        block = p_all.at[block_of(rank, c)]
        for i in range(1, K):
            copy = pltpu.make_async_remote_copy(
                block, block, q_send.at[0, i, c], q_recv.at[rank, c],
                device_id={"spin": lax.rem(k + i, K)}, device_id_type=MESH,
            )
            copy.start()
            sends.append(copy)
    l_all[s] = l_own[...]

    for j in range(1, S):
        other = lax.rem(s + j, S)
        for ref, sem in ((v_all, v_recv), (l_all, l_recv)):
            pltpu.make_async_copy(ref.at[other], ref.at[other], sem.at[other]).wait()

    slab = v_ref.shape[1]
    sites = S * slab
    cells = slab // planes
    fields = [jnp.concatenate([v_all[i, j] for i in range(S)], axis=0) for j in range(6)]
    moved = dot(table_in[: 4 * sites, :], jnp.concatenate(fields, axis=1))

    def field(block, j):
        return moved[block * sites : (block + 1) * sites, j * modes : (j + 1) * modes]

    here = [field(0, j) for j in range(6)]
    link_lines = [l_all[i].astype(F32) for i in range(S)]

    def link(mu, ri, row, column):
        first = (((mu * 2 + ri) * 3 + row) * 3 + column) * cells
        return jnp.concatenate(
            [
                jnp.broadcast_to(line[:, first + cell : first + cell + 1], (planes, modes))
                for line in link_lines
                for cell in range(cells)
            ],
            axis=0,
        )

    columns = []
    for mu in range(3):
        ahead = [field(1 + mu, j) for j in range(6)]
        forward = [0.0] * 6
        adjoint = [0.0] * 6
        for row in range(3):
            for column in range(3):
                real, imag = link(mu, 0, row, column), link(mu, 1, row, column)
                forward[row] += real * ahead[column] - imag * ahead[3 + column]
                forward[3 + row] += real * ahead[3 + column] + imag * ahead[column]
                adjoint[column] += real * here[row] + imag * here[3 + row]
                adjoint[3 + column] += real * here[3 + row] - imag * here[row]
        behind = dot(
            table_in[(4 + mu) * sites : (5 + mu) * sites, :],
            jnp.concatenate([a.astype(BF16) for a in adjoint], axis=1),
        )
        derived = [
            (forward[j] - behind[:, j * modes : (j + 1) * modes]).astype(BF16) for j in range(6)
        ]
        columns.append(jnp.concatenate(derived, axis=0))
        columns.append(jnp.concatenate(derived[3:] + [-d for d in derived[:3]], axis=0))
    norm_scale = 1.0 / math.sqrt(24.0 * sites)
    product = dot(
        jnp.concatenate([h.astype(BF16) for h in here], axis=0),
        jnp.concatenate(columns, axis=1),
        (((0,), (0,)), ((), ())),
    ) * norm_scale
    for mu in range(3):
        for ri in range(2):
            at = (2 * mu + ri) * modes
            e_all[mu, ri] = product[:, at : at + modes]

    def picked(gamma, part):
        return e_all[dirs_ref[gamma], part].astype(BF16).astype(F32)

    e0r, e0i, e1r, e1i, e2r, e2i = [picked(g, part) for g in range(3) for part in range(2)]
    m_ref[...] = jnp.concatenate(
        [
            jnp.concatenate([e2r, e0r + e1i, e2i, e0i - e1r], axis=1),
            jnp.concatenate([e0r - e1i, -e2r, e0i + e1r, -e2i], axis=1),
        ],
        axis=0,
    ).astype(BF16)

    chunks = max(1, rows // CHUNK_ROWS)
    part = rows // chunks
    diagonals = []

    def to_below(source, target, index):
        copy = pltpu.make_async_remote_copy(
            source, target, z_send.at[index], z_recv.at[index],
            device_id={"tm": below}, device_id_type=MESH,
        )
        copy.start()
        return copy

    z_copies = []
    lines = 0.0
    for i in range(chunks):
        span = pl.ds(pl.multiple_of(first_row + i * part, part), part)
        wide = first_rows(p_all[span, :], m_ref[...])
        f_all[span, :] = wide.astype(BF16)
        if i == 0:
            pl.semaphore_wait(ready, 1)
        z_copies.append(to_below(f_all.at[span], f_next.at[pl.ds(i * part, part)], i))
        lines += diagonal_lines(wide, first_row + i * part)
    diagonals.append(lines)

    def arrived(owner, c, sem):
        block = p_all.at[block_of(owner, c)]
        pltpu.make_async_copy(block, block, sem).wait()

    def multiply(owner, c):
        block = block_of(owner, c)
        f_all[block, :] = first_rows(p_all[block, :], m_ref[...]).astype(BF16)

    for i in range(1, K):
        owner = s * K + lax.rem(k + i, K)
        for c in range(PIECES):
            arrived(owner, c, q_recv.at[owner, c])
            multiply(owner, c)
    for c in range(PIECES):
        for j in range(1, S):
            other = lax.rem(s + j, S)
            owner = other * K + k
            arrived(owner, c, p_recv.at[other, c])
            for i in range(1, K):
                block = p_all.at[block_of(owner, c)]
                copy = pltpu.make_async_remote_copy(
                    block, block, q_send.at[j, i, c], q_recv.at[owner, c],
                    device_id={"spin": lax.rem(k + i, K)}, device_id_type=MESH,
                )
                copy.start()
                sends.append(copy)
            multiply(owner, c)
        for j in range(1, S):
            for i in range(1, K):
                owner = lax.rem(s + j, S) * K + lax.rem(k + i, K)
                arrived(owner, c, q_recv.at[owner, c])
                multiply(owner, c)

    lane = lax.broadcasted_iota(jnp.int32, (2, 128), 1)
    wanted = jnp.full((2, 128), -1, jnp.int32)
    for n in range(src_ref.shape[0]):
        wanted = jnp.where(lane == n, src_ref[n], wanted)
    tile_row = lax.broadcasted_iota(jnp.int32, (8, 128), 0)
    weight = jnp.zeros((8, 128), F32)
    for o in range(3):
        count = sum(jnp.where(off_ref[j] == o, 1, 0) for j in range(off_ref.shape[0]))
        weight = jnp.where(lax.div(tile_row, 2) == o, count.astype(F32), weight)

    lines = 0.0
    for i in range(chunks):
        span = pl.ds(i * part, part)
        z_copies[i].wait_recv()
        wide = complex_rows(f_next[span, :], f_all[...])
        s_own[span, :] = wide.astype(BF16)
        z_copies.append(to_below(s_own.at[span], s_next.at[span], chunks + i))
        lines += diagonal_lines(wide, first_row + i * part)
    diagonals.append(lines)

    share, half = elem_ref.shape[0], elem_ref.shape[3]
    own_rows = pl.ds(pl.multiple_of(s * share, share), share)
    for mu in range(3):
        for ri in range(2):
            block = e_all[mu, ri, own_rows, :]
            mine_columns = block[:, :half]
            for i in range(1, K):
                mine_columns = jnp.where(k == i, block[:, i * half : (i + 1) * half], mine_columns)
            elem_ref[:, mu, ri, :] = mine_columns

    lines = 0.0
    for i in range(chunks):
        span = pl.ds(i * part, part)
        z_copies[chunks + i].wait_recv()
        wide = complex_rows(s_next[span, :], f_all[...])
        chain_ref[span, :] = (wide * math.sqrt(order)).astype(BF16)
        lines += diagonal_lines(wide, first_row + i * part)
    diagonals.append(lines)

    t_all[t * G + rank] = jnp.concatenate(diagonals + [jnp.zeros((2, 128), F32)], axis=0)
    total = T * G
    me = t * G + rank

    def trace_copy(j):
        other = lax.rem(me + j, total)
        group = lax.rem(other, G)
        return other, pltpu.make_async_remote_copy(
            t_all.at[me], t_all.at[me], t_send.at[j], t_recv.at[me],
            device_id={
                "tm": lax.div(other, G), "space": lax.div(group, K), "spin": lax.rem(group, K)
            },
            device_id_type=MESH,
        )

    def start_trace(j, carry):
        trace_copy(j)[1].start()
        return carry

    lax.fori_loop(1, total, start_trace, 0)

    def wait_trace(j, carry):
        other, copy = trace_copy(j)
        copy.wait_send()
        pltpu.make_async_copy(t_all.at[other], t_all.at[other], t_recv.at[other]).wait()
        return carry

    lax.fori_loop(1, total, wait_trace, 0)

    def add_time(i, acc):
        summed = t_all[i * G]
        for g in range(1, G):
            summed = summed + t_all[i * G + g]
        weighted = jnp.sum(summed * weight, axis=1, keepdims=True)
        pair = weighted[0:2] + weighted[2:4] + weighted[4:6]
        return acc + jnp.where(wanted == i, pair, 0.0)

    found = lax.fori_loop(0, T, add_time, jnp.zeros((2, 128), F32))
    corr_ref[...] = found[:, : corr_ref.shape[1]]

    for copy in sends:
        copy.wait_send()
    for copy in z_copies:
        copy.wait_send()


def copy_kernel(*refs):
    copies = [
        pltpu.make_async_copy(refs[i], refs[3 + i], refs[6].at[i]) for i in range(3)
    ]
    for copy in copies:
        copy.start()
    for copy in copies:
        copy.wait()


def on_device(
    sizes, eigenvectors, gauge_links, perambulators, source_times, insert_offsets, derivative_dirs
):
    T, S, K = sizes
    _, _, _, planes, side, _, modes = eigenvectors.shape
    slab = planes * side * side
    vectors = eigenvectors.reshape((6, slab, modes))
    links = jnp.swapaxes(gauge_links, 5, 6).reshape((54 * side * side, planes))
    peram = perambulators[0]
    rows, width = peram.shape
    order = width // 2
    chunks = max(1, rows // CHUNK_ROWS)
    table = jnp.asarray(shift_table(S, planes, side), BF16)
    vmem = pl.BlockSpec(memory_space=pltpu.VMEM)
    hbm = pl.BlockSpec(memory_space=pltpu.HBM)
    smem = pl.BlockSpec(memory_space=pltpu.SMEM)
    dma = pltpu.SemaphoreType.DMA
    elementals, chain, correlator = pl.pallas_call(
        functools.partial(kernel, sizes),
        out_shape=(
            pltpu.VMEM((modes // S, 3, 2, modes // K), F32),
            pltpu.VMEM((rows, width), BF16),
            pltpu.VMEM((2, source_times.shape[0]), F32),
        ),
        in_specs=[hbm, hbm, hbm, hbm, smem, smem, smem],
        out_specs=(vmem, vmem, vmem),
        scratch_shapes=[
            pltpu.VMEM(links.shape, BF16),
            pltpu.VMEM(table.shape, BF16),
            dma((4,)),
            pltpu.VMEM((S, 6, slab, modes), BF16),
            pltpu.VMEM((planes, 54 * side * side), BF16),
            pltpu.VMEM((S, planes, 54 * side * side), BF16),
            pltpu.VMEM((order, width), BF16),
            pltpu.VMEM((3, 2, modes, modes), F32),
            pltpu.VMEM((2 * modes, 4 * modes), BF16),
            pltpu.VMEM((order, width), BF16),
            pltpu.VMEM((rows, width), BF16),
            pltpu.VMEM((rows, width), BF16),
            pltpu.VMEM((rows, width), BF16),
            pltpu.VMEM((T * S * K, 8, 128), F32),
            dma((S,)),
            dma((S,)),
            dma((S,)),
            dma((S,)),
            dma((S, PIECES)),
            dma((S, PIECES)),
            dma((S, K, PIECES)),
            dma((S * K, PIECES)),
            pltpu.SemaphoreType.REGULAR,
            dma((2 * chunks,)),
            dma((2 * chunks,)),
            dma((T * S * K,)),
            dma((T * S * K,)),
        ],
        compiler_params=pltpu.CompilerParams(collective_id=0, has_side_effects=True),
    )(vectors, links, peram, table, source_times, insert_offsets, derivative_dirs)
    elementals, chain, correlator = pl.pallas_call(
        copy_kernel,
        out_shape=tuple(jax.ShapeDtypeStruct(a.shape, a.dtype) for a in (elementals, chain, correlator)),
        in_specs=[vmem] * 3,
        out_specs=(pl.BlockSpec(memory_space=pl.ANY),) * 3,
        scratch_shapes=[dma((3,))],
    )(*(pltpu.with_memory_space_constraint(a, pltpu.VMEM) for a in (elementals, chain, correlator)))
    return (elementals[None], chain[None], correlator.T)


def solution(mesh):
    sizes = (mesh.shape["tm"], mesh.shape["space"], mesh.shape["spin"])
    in_specs = (
        P(("cfg", "tm"), None, None, "space", None, None, None),
        P(("cfg", "tm"), None, None, None, None, "space", None),
        P(("cfg", "tm"), ("space", "spin"), None),
        P(),
        P(),
        P(),
    )
    out_specs = (
        P(("cfg", "tm"), "space", None, None, "spin"),
        P(("cfg", "tm"), ("space", "spin"), None),
        P("cfg", None),
    )
    return jax.shard_map(
        functools.partial(on_device, sizes),
        mesh=mesh,
        in_specs=in_specs,
        out_specs=out_specs,
        check_vma=False,
    )
```

```python
import functools
import math

import jax
import jax.numpy as jnp
import numpy as np
from jax import lax
from jax.experimental import pallas as pl
from jax.experimental.pallas import tpu as pltpu
from jax.sharding import PartitionSpec as P

MESH = pl.DeviceIdType.MESH
F32 = jnp.float32
BF16 = jnp.bfloat16
CHUNK_ROWS = 16
PIECES = 4


def dot(a, b, dims=(((1,), (0,)), ((), ()))):
    return lax.dot_general(a, b, dims, preferred_element_type=F32)


def shift_table(slabs, planes, side):
    depth, area = slabs * planes, side * side
    slab, cell, plane = np.meshgrid(
        np.arange(slabs), np.arange(area), np.arange(planes), indexing="ij"
    )
    z, y, x = (slab * planes + plane).ravel(), (cell // side).ravel(), (cell % side).ravel()
    count = z.size

    def plain(z, y, x):
        return ((z % depth) * side + y % side) * side + x % side

    def ordered(z, y, x):
        z = z % depth
        return ((z // planes) * area + (y % side) * side + x % side) * planes + z % planes

    targets = [
        plain(z, y, x), plain(z, y, x + 1), plain(z, y + 1, x), plain(z + 1, y, x),
        ordered(z, y, x - 1), ordered(z, y - 1, x), ordered(z - 1, y, x),
    ]
    table = np.zeros((len(targets) * count, count), np.float32)
    for block, target in enumerate(targets):
        table[block * count + np.arange(count), target] = 1.0
    return table


def diagonal_lines(product, first_row, lanes=128):
    rows, width = product.shape
    order = width // 2
    hit = lax.broadcasted_iota(jnp.int32, (rows, order), 1) == (
        first_row + lax.broadcasted_iota(jnp.int32, (rows, order), 0)
    )
    lines = []
    for half in (product[:, :order], product[:, order:]):
        kept = jnp.where(hit, half, 0.0)
        folded = sum(kept[:, i : i + lanes] for i in range(0, order, lanes))
        lines.append(jnp.sum(folded, axis=0, keepdims=True))
    return jnp.concatenate(lines, axis=0)


def complex_rows(left, right):
    rows, width = left.shape
    order = width // 2
    both = dot(jnp.concatenate([left[:, :order], left[:, order:]], axis=0), right)
    top, bottom = both[:rows], both[rows:]
    return jnp.concatenate(
        [top[:, :order] - bottom[:, order:], top[:, order:] + bottom[:, :order]], axis=1
    )


def first_rows(peram, mixed):
    rows, width = peram.shape
    order = width // 2
    half = order // 2
    stacked = jnp.concatenate(
        [
            peram[:, half:order],
            peram[:, order + half :],
            peram[:, :half],
            peram[:, order : order + half],
        ],
        axis=0,
    )
    y = dot(stacked, mixed)
    down_real = y[:rows, :half] - y[rows : 2 * rows, half:]
    down_imag = y[:rows, half:] + y[rows : 2 * rows, :half]
    up_real = y[2 * rows : 3 * rows, :half] - y[3 * rows :, half:]
    up_imag = y[2 * rows : 3 * rows, half:] + y[3 * rows :, :half]
    return jnp.concatenate([-down_imag, up_imag, down_real, -up_real], axis=1) * (
        1.0 / math.sqrt(order)
    )


def kernel(
    sizes,
    v_ref,
    l_ref,
    p_ref,
    table_ref,
    src_ref,
    off_ref,
    dirs_ref,
    elem_ref,
    chain_ref,
    corr_ref,
    l_in,
    table_in,
    in_sem,
    v_all,
    l_own,
    l_all,
    p_all,
    e_all,
    m_ref,
    f_all,
    f_next,
    s_own,
    s_next,
    t_all,
    v_send,
    v_recv,
    l_send,
    l_recv,
    p_send,
    p_recv,
    q_send,
    q_recv,
    ready,
    z_send,
    z_recv,
    t_send,
    t_recv,
):
    T, S, K = sizes
    G = S * K
    t, s, k = lax.axis_index("tm"), lax.axis_index("space"), lax.axis_index("spin")
    rank = s * K + k
    rows = p_ref.shape[0]
    order = p_ref.shape[1] // 2
    modes = v_ref.shape[2]
    first_row = rank * rows
    mine = pl.ds(pl.multiple_of(first_row, rows), rows)
    below, above = lax.rem(t + T - 1, T), lax.rem(t + 1, T)

    loads = [
        pltpu.make_async_copy(source, target, in_sem.at[i])
        for i, (source, target) in enumerate(
            (
                (l_ref, l_in),
                (v_ref, v_all.at[s]),
                (p_ref, p_all.at[mine]),
                (table_ref, table_in),
            )
        )
    ]
    for load in loads:
        load.start()
    planes = l_ref.shape[1]
    barrier = pltpu.get_barrier_semaphore()
    for j in range(1, G):
        other = lax.rem(rank + j, G)
        pl.semaphore_signal(
            barrier,
            inc=1,
            device_id={"tm": t, "space": lax.div(other, K), "spin": lax.rem(other, K)},
            device_id_type=MESH,
        )
    pl.semaphore_signal(barrier, inc=1, device_id={"tm": below}, device_id_type=MESH)
    entered = G
    if T > 4:
        def announce(j, carry):
            other = lax.rem(t * G + rank + j, T * G)
            group = lax.rem(other, G)
            pl.semaphore_signal(
                barrier,
                inc=1,
                device_id={
                    "tm": lax.div(other, G), "space": lax.div(group, K), "spin": lax.rem(group, K)
                },
                device_id_type=MESH,
            )
            return carry

        lax.fori_loop(1, T * G, announce, 0)
        entered += T * G - 1
    eye = (
        lax.broadcasted_iota(jnp.int32, (planes, planes), 0)
        == lax.broadcasted_iota(jnp.int32, (planes, planes), 1)
    ).astype(F32).astype(BF16)
    loads[0].wait()
    l_own[...] = dot(eye, l_in[...], (((1,), (1,)), ((), ()))).astype(BF16)
    for load in loads[1:]:
        load.wait()
    pl.semaphore_wait(barrier, entered)
    pl.semaphore_signal(ready, inc=1, device_id={"tm": above}, device_id_type=MESH)

    sends = []
    for j in range(1, S):
        other = lax.rem(s + j, S)
        for source, target, send_sem, recv_sem in (
            (v_all.at[s], v_all.at[s], v_send, v_recv),
            (l_own, l_all.at[s], l_send, l_recv),
        ):
            copy = pltpu.make_async_remote_copy(
                source, target, send_sem.at[j], recv_sem.at[s],
                device_id={"space": other}, device_id_type=MESH,
            )
            copy.start()
            sends.append(copy)
    piece = rows // PIECES

    def block_of(owner, c):
        return pl.ds(pl.multiple_of(owner * rows + c * piece, piece), piece)

    for c in range(PIECES):
        block = p_all.at[block_of(rank, c)]
        for j in range(1, S):
            copy = pltpu.make_async_remote_copy(
                block, block, p_send.at[j, c], p_recv.at[s, c],
                device_id={"space": lax.rem(s + j, S)}, device_id_type=MESH,
            )
            copy.start()
            sends.append(copy)
    for c in range(PIECES):
        block = p_all.at[block_of(rank, c)]
        for i in range(1, K):
            copy = pltpu.make_async_remote_copy(
                block, block, q_send.at[0, i, c], q_recv.at[rank, c],
                device_id={"spin": lax.rem(k + i, K)}, device_id_type=MESH,
            )
            copy.start()
            sends.append(copy)
    l_all[s] = l_own[...]

    for j in range(1, S):
        other = lax.rem(s + j, S)
        for ref, sem in ((v_all, v_recv), (l_all, l_recv)):
            pltpu.make_async_copy(ref.at[other], ref.at[other], sem.at[other]).wait()

    slab = v_ref.shape[1]
    sites = S * slab
    cells = slab // planes
    fields = [jnp.concatenate([v_all[i, j] for i in range(S)], axis=0) for j in range(6)]
    moved = dot(table_in[: 4 * sites, :], jnp.concatenate(fields, axis=1))

    def field(block, j):
        return moved[block * sites : (block + 1) * sites, j * modes : (j + 1) * modes]

    here = [field(0, j) for j in range(6)]
    link_lines = [l_all[i].astype(F32) for i in range(S)]

    def link(mu, ri, row, column):
        first = (((mu * 2 + ri) * 3 + row) * 3 + column) * cells
        return jnp.concatenate(
            [
                jnp.broadcast_to(line[:, first + cell : first + cell + 1], (planes, modes))
                for line in link_lines
                for cell in range(cells)
            ],
            axis=0,
        )

    columns = []
    for mu in range(3):
        ahead = [field(1 + mu, j) for j in range(6)]
        forward = [0.0] * 6
        adjoint = [0.0] * 6
        for row in range(3):
            for column in range(3):
                real, imag = link(mu, 0, row, column), link(mu, 1, row, column)
                forward[row] += real * ahead[column] - imag * ahead[3 + column]
                forward[3 + row] += real * ahead[3 + column] + imag * ahead[column]
                adjoint[column] += real * here[row] + imag * here[3 + row]
                adjoint[3 + column] += real * here[3 + row] - imag * here[row]
        behind = dot(
            table_in[(4 + mu) * sites : (5 + mu) * sites, :],
            jnp.concatenate([a.astype(BF16) for a in adjoint], axis=1),
        )
        derived = [
            (forward[j] - behind[:, j * modes : (j + 1) * modes]).astype(BF16) for j in range(6)
        ]
        columns.append(jnp.concatenate(derived, axis=0))
        columns.append(jnp.concatenate(derived[3:] + [-d for d in derived[:3]], axis=0))
    norm_scale = 1.0 / math.sqrt(24.0 * sites)
    product = dot(
        jnp.concatenate([h.astype(BF16) for h in here], axis=0),
        jnp.concatenate(columns, axis=1),
        (((0,), (0,)), ((), ())),
    ) * norm_scale
    for mu in range(3):
        for ri in range(2):
            at = (2 * mu + ri) * modes
            e_all[mu, ri] = product[:, at : at + modes]

    def picked(gamma, part):
        return e_all[dirs_ref[gamma], part].astype(BF16).astype(F32)

    e0r, e0i, e1r, e1i, e2r, e2i = [picked(g, part) for g in range(3) for part in range(2)]
    m_ref[...] = jnp.concatenate(
        [
            jnp.concatenate([e2r, e0r + e1i, e2i, e0i - e1r], axis=1),
            jnp.concatenate([e0r - e1i, -e2r, e0i + e1r, -e2i], axis=1),
        ],
        axis=0,
    ).astype(BF16)

    chunks = max(1, rows // CHUNK_ROWS)
    part = rows // chunks
    diagonals = []

    def to_below(source, target, index):
        copy = pltpu.make_async_remote_copy(
            source, target, z_send.at[index], z_recv.at[index],
            device_id={"tm": below}, device_id_type=MESH,
        )
        copy.start()
        return copy

    z_copies = []
    lines = 0.0
    for i in range(chunks):
        span = pl.ds(pl.multiple_of(first_row + i * part, part), part)
        wide = first_rows(p_all[span, :], m_ref[...])
        f_all[span, :] = wide.astype(BF16)
        if i == 0:
            pl.semaphore_wait(ready, 1)
        z_copies.append(to_below(f_all.at[span], f_next.at[pl.ds(i * part, part)], i))
        lines += diagonal_lines(wide, first_row + i * part)
    diagonals.append(lines)

    def arrived(owner, c, sem):
        block = p_all.at[block_of(owner, c)]
        pltpu.make_async_copy(block, block, sem).wait()

    def multiply(owner, c):
        block = block_of(owner, c)
        f_all[block, :] = first_rows(p_all[block, :], m_ref[...]).astype(BF16)

    for i in range(1, K):
        owner = s * K + lax.rem(k + i, K)
        for c in range(PIECES):
            arrived(owner, c, q_recv.at[owner, c])
            multiply(owner, c)
    for c in range(PIECES):
        for j in range(1, S):
            other = lax.rem(s + j, S)
            owner = other * K + k
            arrived(owner, c, p_recv.at[other, c])
            for i in range(1, K):
                block = p_all.at[block_of(owner, c)]
                copy = pltpu.make_async_remote_copy(
                    block, block, q_send.at[j, i, c], q_recv.at[owner, c],
                    device_id={"spin": lax.rem(k + i, K)}, device_id_type=MESH,
                )
                copy.start()
                sends.append(copy)
            multiply(owner, c)
        for j in range(1, S):
            for i in range(1, K):
                owner = lax.rem(s + j, S) * K + lax.rem(k + i, K)
                arrived(owner, c, q_recv.at[owner, c])
                multiply(owner, c)

    lane = lax.broadcasted_iota(jnp.int32, (2, 128), 1)
    wanted = jnp.full((2, 128), -1, jnp.int32)
    for n in range(src_ref.shape[0]):
        wanted = jnp.where(lane == n, src_ref[n], wanted)
    tile_row = lax.broadcasted_iota(jnp.int32, (8, 128), 0)
    weight = jnp.zeros((8, 128), F32)
    for o in range(3):
        count = sum(jnp.where(off_ref[j] == o, 1, 0) for j in range(off_ref.shape[0]))
        weight = jnp.where(lax.div(tile_row, 2) == o, count.astype(F32), weight)

    lines = 0.0
    for i in range(chunks):
        span = pl.ds(i * part, part)
        z_copies[i].wait_recv()
        wide = complex_rows(f_next[span, :], f_all[...])
        s_own[span, :] = wide.astype(BF16)
        z_copies.append(to_below(s_own.at[span], s_next.at[span], chunks + i))
        lines += diagonal_lines(wide, first_row + i * part)
    diagonals.append(lines)

    share, half = elem_ref.shape[0], elem_ref.shape[3]
    own_rows = pl.ds(pl.multiple_of(s * share, share), share)
    for mu in range(3):
        for ri in range(2):
            block = e_all[mu, ri, own_rows, :]
            mine_columns = block[:, :half]
            for i in range(1, K):
                mine_columns = jnp.where(k == i, block[:, i * half : (i + 1) * half], mine_columns)
            elem_ref[:, mu, ri, :] = mine_columns

    lines = 0.0
    for i in range(chunks):
        span = pl.ds(i * part, part)
        z_copies[chunks + i].wait_recv()
        wide = complex_rows(s_next[span, :], f_all[...])
        chain_ref[span, :] = (wide * math.sqrt(order)).astype(BF16)
        lines += diagonal_lines(wide, first_row + i * part)
    diagonals.append(lines)

    t_all[t * G + rank] = jnp.concatenate(diagonals + [jnp.zeros((2, 128), F32)], axis=0)
    total = T * G
    me = t * G + rank

    def trace_copy(j):
        other = lax.rem(me + j, total)
        group = lax.rem(other, G)
        return other, pltpu.make_async_remote_copy(
            t_all.at[me], t_all.at[me], t_send.at[j], t_recv.at[me],
            device_id={
                "tm": lax.div(other, G), "space": lax.div(group, K), "spin": lax.rem(group, K)
            },
            device_id_type=MESH,
        )

    if total <= 16:

        def wrapped(value, size):
            return jnp.where(value >= size, value - size, value)

        started = []
        for j in range(1, total):
            at = (
                wrapped(t + j // G, T), wrapped(s + (j % G) // K, S), wrapped(k + j % K, K)
            )
            copy = pltpu.make_async_remote_copy(
                t_all.at[me], t_all.at[me], t_send.at[j], t_recv.at[me],
                device_id=dict(zip(("tm", "space", "spin"), at)), device_id_type=MESH,
            )
            copy.start()
            started.append((copy, (at[0] * S + at[1]) * K + at[2]))
        for copy, other in started:
            copy.wait_send()
            pltpu.make_async_copy(t_all.at[other], t_all.at[other], t_recv.at[other]).wait()
    else:
        def start_trace(j, carry):
            trace_copy(j)[1].start()
            return carry

        lax.fori_loop(1, total, start_trace, 0)

        def wait_trace(j, carry):
            other, copy = trace_copy(j)
            copy.wait_send()
            pltpu.make_async_copy(t_all.at[other], t_all.at[other], t_recv.at[other]).wait()
            return carry

        lax.fori_loop(1, total, wait_trace, 0)

    def add_time(i, acc):
        summed = t_all[i * G]
        for g in range(1, G):
            summed = summed + t_all[i * G + g]
        weighted = jnp.sum(summed * weight, axis=1, keepdims=True)
        pair = weighted[0:2] + weighted[2:4] + weighted[4:6]
        return acc + jnp.where(wanted == i, pair, 0.0)

    found = lax.fori_loop(0, T, add_time, jnp.zeros((2, 128), F32))
    corr_ref[...] = found[:, : corr_ref.shape[1]]

    for copy in sends:
        copy.wait_send()
    for copy in z_copies:
        copy.wait_send()


def copy_kernel(*refs):
    copies = [
        pltpu.make_async_copy(refs[i], refs[3 + i], refs[6].at[i]) for i in range(3)
    ]
    for copy in copies:
        copy.start()
    for copy in copies:
        copy.wait()


def on_device(
    sizes, eigenvectors, gauge_links, perambulators, source_times, insert_offsets, derivative_dirs
):
    T, S, K = sizes
    _, _, _, planes, side, _, modes = eigenvectors.shape
    slab = planes * side * side
    vectors = eigenvectors.reshape((6, slab, modes))
    links = jnp.swapaxes(gauge_links, 5, 6).reshape((54 * side * side, planes))
    peram = perambulators[0]
    rows, width = peram.shape
    order = width // 2
    chunks = max(1, rows // CHUNK_ROWS)
    table = jnp.asarray(shift_table(S, planes, side), BF16)
    vmem = pl.BlockSpec(memory_space=pltpu.VMEM)
    hbm = pl.BlockSpec(memory_space=pltpu.HBM)
    smem = pl.BlockSpec(memory_space=pltpu.SMEM)
    dma = pltpu.SemaphoreType.DMA
    elementals, chain, correlator = pl.pallas_call(
        functools.partial(kernel, sizes),
        out_shape=(
            pltpu.VMEM((modes // S, 3, 2, modes // K), F32),
            pltpu.VMEM((rows, width), BF16),
            pltpu.VMEM((2, source_times.shape[0]), F32),
        ),
        in_specs=[hbm, hbm, hbm, hbm, smem, smem, smem],
        out_specs=(vmem, vmem, vmem),
        scratch_shapes=[
            pltpu.VMEM(links.shape, BF16),
            pltpu.VMEM(table.shape, BF16),
            dma((4,)),
            pltpu.VMEM((S, 6, slab, modes), BF16),
            pltpu.VMEM((planes, 54 * side * side), BF16),
            pltpu.VMEM((S, planes, 54 * side * side), BF16),
            pltpu.VMEM((order, width), BF16),
            pltpu.VMEM((3, 2, modes, modes), F32),
            pltpu.VMEM((2 * modes, 4 * modes), BF16),
            pltpu.VMEM((order, width), BF16),
            pltpu.VMEM((rows, width), BF16),
            pltpu.VMEM((rows, width), BF16),
            pltpu.VMEM((rows, width), BF16),
            pltpu.VMEM((T * S * K, 8, 128), F32),
            dma((S,)),
            dma((S,)),
            dma((S,)),
            dma((S,)),
            dma((S, PIECES)),
            dma((S, PIECES)),
            dma((S, K, PIECES)),
            dma((S * K, PIECES)),
            pltpu.SemaphoreType.REGULAR,
            dma((2 * chunks,)),
            dma((2 * chunks,)),
            dma((T * S * K,)),
            dma((T * S * K,)),
        ],
        compiler_params=pltpu.CompilerParams(collective_id=0, has_side_effects=True),
    )(vectors, links, peram, table, source_times, insert_offsets, derivative_dirs)
    elementals, chain, correlator = pl.pallas_call(
        copy_kernel,
        out_shape=tuple(jax.ShapeDtypeStruct(a.shape, a.dtype) for a in (elementals, chain, correlator)),
        in_specs=[vmem] * 3,
        out_specs=(pl.BlockSpec(memory_space=pl.ANY),) * 3,
        scratch_shapes=[dma((3,))],
    )(*(pltpu.with_memory_space_constraint(a, pltpu.VMEM) for a in (elementals, chain, correlator)))
    return (elementals[None], chain[None], correlator.T)


def solution(mesh):
    sizes = (mesh.shape["tm"], mesh.shape["space"], mesh.shape["spin"])
    in_specs = (
        P(("cfg", "tm"), None, None, "space", None, None, None),
        P(("cfg", "tm"), None, None, None, None, "space", None),
        P(("cfg", "tm"), ("space", "spin"), None),
        P(),
        P(),
        P(),
    )
    out_specs = (
        P(("cfg", "tm"), "space", None, None, "spin"),
        P(("cfg", "tm"), ("space", "spin"), None),
        P("cfg", None),
    )
    return jax.shard_map(
        functools.partial(on_device, sizes),
        mesh=mesh,
        in_specs=in_specs,
        out_specs=out_specs,
        check_vma=False,
    )
```
